256 devices in a mesh: fsdp: 2 (over y_hi), dp: 32 (over x, z), owner: 4 (over y_lo, core).
Axes of the slice: x: 4, y: 4 (y_hi: 2, y_lo: 2; y = y_hi * 2 + y_lo), z: 8, core: 2. Of those that a mesh axis runs over, the one named last changes fastest.
Arguments:
- hidden: bfloat16 [256, 256, 4096], P(('fsdp', 'dp', 'owner')), may hold values from -6 to 6
- norm_gain: float32 [4096], replicated, may hold values from 0.1 to 1.9
- query_weight: bfloat16 [4096, 2048], P(('fsdp', 'dp')), may hold values from -0.09375 to 0.09375
- key_value_weight: bfloat16 [4096, 1024], P(('fsdp', 'dp')), may hold values from -0.09375 to 0.09375
- lengths: int32 [256], P(('fsdp', 'dp', 'owner')), may hold values from 128 to 256, as said below
- cotangent: bfloat16 [256, 256, 2048], P(('fsdp', 'dp', 'owner')), may hold values from -6 to 6
- cartridge: float32 [512, 1024], P('owner'), may hold values from -48 to 48
- adam_first_moment: float32 [512, 1024], P('owner'), may hold values from -6 to 6
- adam_second_moment: float32 [512, 1024], P('owner'), may hold values from 0.01 to 1
Outputs:
- attention_out: bfloat16 [256, 256, 2048], P(('fsdp', 'dp', 'owner'))
- new_cartridge: float32 [512, 1024], P('owner')
- new_first: float32 [512, 1024], P('owner')
- new_second: float32 [512, 1024], P('owner')
The draws below stay inside these ranges and needn't reach their ends.
Inputs may be any that keep to these rules, and one draw needn't show every extreme that they name: `lengths`: each conversation's live tokens are its first rows; the rows after them are padding; some conversation is full.
All inputs are finite; a program needn't handle non-finite values.
Results may differ from the reference program's by a relative error of at most 0.008.
The reference program's roundings to bfloat16 on the way count: a program that leaves them out, or rounds other values in their place, can miss the bound.
Values may be sent and summed in bfloat16 or wider, within the bound.
No kernel may reach another device: no remote copies, remote signals or barrier semaphores. Data moves between devices by JAX's collectives and lax.ppermute only.
A program may use at most 128 MiB of HBM per device.

```python
import math
import jax
import jax.numpy as jnp
from jax import lax

MODEL_WIDTH = 4096
HEAD_SIZE = 128
QUERY_HEADS = 16
KEY_VALUE_HEADS = 4
S = 256
STEP = 50
PREFIX_TOKENS = 512
CONVS = 256


def draw_lengths(key, part):
    counts = jax.random.randint(jax.random.fold_in(key, 11), (CONVS,), S // 2, S + 1, dtype=jnp.int32)
    full_index = jax.random.randint(jax.random.fold_in(key, 12), (), 0, CONVS, dtype=jnp.int32)
    short_index = (full_index + jax.random.randint(jax.random.fold_in(key, 13), (), 1, CONVS, dtype=jnp.int32)) % CONVS
    places = jnp.arange(CONVS, dtype=jnp.int32)
    counts = jnp.where(places == full_index, S, counts)
    counts = jnp.where(places == short_index, S // 2, counts)
    return counts.astype(jnp.int32)


def draw_cartridge(key, part):
    column_count = 2 * KEY_VALUE_HEADS * HEAD_SIZE
    return jnp.clip(2.0 * jax.random.normal(jax.random.fold_in(key, 24), (PREFIX_TOKENS, column_count), jnp.float32), -8.0, 8.0)


def level_of(own_key, shape, shards, low, high):
    def one(axis_at, shards_of):
        steps = jax.random.uniform(jax.random.fold_in(jax.random.fold_in(own_key, 6), axis_at), (shards_of,), jnp.float32, low / len(shards), high / len(shards))
        return jnp.repeat(jnp.exp(steps), shape[axis_at] // shards_of).reshape((-1,) + (1,) * (len(shape) - axis_at - 1))

    loudness = one(*shards[0])
    for cut in shards[1:]:
        loudness = loudness * one(*cut)
    return loudness


def bell_draw(key, dims, scale, reach, cuts=(), kind=jnp.bfloat16):
    drawn = jax.random.normal(key, dims, jnp.float32) * scale
    if len(cuts) > 0:
        drawn = level_of(key, dims, cuts, -0.22, 0.18) * drawn
    return jnp.clip(drawn, min=-reach, max=reach).astype(kind)


def setup_inputs(seed: int = 0) -> dict:
    arg_keys = jax.random.split(jax.random.key(seed), 10)
    hidden = bell_draw(arg_keys[0], (CONVS, S, MODEL_WIDTH), 1.0, 6.0, ((0, 256),))
    norm_gain = jnp.clip(1.0 + 0.18 * jax.random.normal(arg_keys[1], (MODEL_WIDTH,), jnp.float32), 0.1, 1.9)
    query_weight = bell_draw(arg_keys[2], (MODEL_WIDTH, QUERY_HEADS * HEAD_SIZE), MODEL_WIDTH ** -0.5, 0.09375, ((0, 64),))
    key_value_weight = bell_draw(arg_keys[3], (MODEL_WIDTH, 2 * KEY_VALUE_HEADS * HEAD_SIZE), MODEL_WIDTH ** -0.5, 0.09375, ((0, 64),))
    lengths = draw_lengths(jax.random.fold_in(arg_keys[9], 71), 0)
    cotangent = bell_draw(arg_keys[5], (CONVS, S, QUERY_HEADS * HEAD_SIZE), 1.0, 6.0, ((0, 256),))
    cartridge = draw_cartridge(jax.random.fold_in(arg_keys[9], 71), 0)
    adam_first_moment = bell_draw(arg_keys[7], (PREFIX_TOKENS, 2 * KEY_VALUE_HEADS * HEAD_SIZE), 1.0, 6.0, ((0, 4),), jnp.float32)
    adam_second_moment = jnp.clip(jnp.exp(math.log(1.0) - 4.6051702 * jax.random.uniform(arg_keys[8], (PREFIX_TOKENS, 2 * KEY_VALUE_HEADS * HEAD_SIZE), jnp.float32) ** level_of(arg_keys[8], (PREFIX_TOKENS, 2 * KEY_VALUE_HEADS * HEAD_SIZE), ((0, 4),), -0.2, 0.2)), 0.01, 1.0)
    return dict(hidden=hidden, norm_gain=norm_gain, query_weight=query_weight, key_value_weight=key_value_weight, lengths=lengths, cotangent=cotangent, cartridge=cartridge, adam_first_moment=adam_first_moment, adam_second_moment=adam_second_moment)


def rotary_heads(values, offset):
    sequence_rows = values.shape[0]
    half_size = values.shape[2] // 2
    exponent = jnp.arange(half_size, dtype=jnp.float32) * (2.0 / values.shape[2])
    inverse = jnp.power(jnp.float32(500000.0), -exponent)
    position = (offset + jnp.arange(sequence_rows)).astype(jnp.float32)
    angles = position[:, None] * inverse[None, :]
    cosine = jnp.cos(angles)[:, None, :]
    sine = jnp.sin(angles)[:, None, :]
    first_half = values[..., :half_size]
    second_half = values[..., half_size:]
    return jnp.concatenate([first_half * cosine - second_half * sine, second_half * cosine + first_half * sine], axis=-1)

def adam_update(current, moment_one, moment_two, prefix_gradient):
    one_new = 0.9 * moment_one + 0.1 * prefix_gradient
    two_new = 0.999 * moment_two + 0.001 * prefix_gradient * prefix_gradient
    one_fix = 1.0 - 0.9 ** STEP
    two_fix = 1.0 - 0.999 ** STEP
    updated = current - 0.02 * (one_new / one_fix) / (jnp.sqrt(two_new / two_fix) + 1e-08)
    return (updated, one_new, two_new)

def one_conversation(states, length, upstream_unshaped, cartridge_keys, cartridge_values, query_weight, key_value_weight, norm_gain):
    sequence_rows = states.shape[0]
    query_group_size = QUERY_HEADS // KEY_VALUE_HEADS
    score_scale = HEAD_SIZE ** (-0.5)
    wide = states.astype(jnp.float32)
    normed = (wide * lax.rsqrt(lax.optimization_barrier(jnp.mean(wide * wide, axis=1, keepdims=True)) + 1e-05) * norm_gain).astype(jnp.bfloat16)
    proj_query = jnp.dot(normed, query_weight, preferred_element_type=jnp.float32)
    project_key_value = jnp.dot(normed, key_value_weight, preferred_element_type=jnp.float32)
    query_rows = rotary_heads(proj_query.reshape(sequence_rows, QUERY_HEADS, HEAD_SIZE), PREFIX_TOKENS).astype(jnp.bfloat16)
    sequence_keys = rotary_heads(project_key_value[:, :KEY_VALUE_HEADS * HEAD_SIZE].reshape(sequence_rows, KEY_VALUE_HEADS, HEAD_SIZE), PREFIX_TOKENS).astype(jnp.bfloat16)
    sequence_values = project_key_value[:, KEY_VALUE_HEADS * HEAD_SIZE:].reshape(sequence_rows, KEY_VALUE_HEADS, HEAD_SIZE).astype(jnp.bfloat16)
    grouped_heads = query_rows.reshape(sequence_rows, KEY_VALUE_HEADS, query_group_size, HEAD_SIZE).astype(jnp.float32)
    keys_wide = cartridge_keys.astype(jnp.float32)
    values_wide = cartridge_values.astype(jnp.float32)
    pre_scores = jnp.einsum('shgd,phd->hgsp', grouped_heads, keys_wide) * score_scale
    own_scores = jnp.einsum('shgd,thd->hgst', grouped_heads, sequence_keys.astype(jnp.float32)) * score_scale
    causal = jnp.arange(sequence_rows)[:, None] >= jnp.arange(sequence_rows)[None, :]
    own_scores = jnp.where(causal, own_scores, -jnp.inf)
    joined = jnp.concatenate([pre_scores, own_scores], axis=-1)
    probs = jax.nn.softmax(joined, axis=-1)
    pre_probs = probs[..., :PREFIX_TOKENS]
    probs_low = probs.astype(jnp.bfloat16).astype(jnp.float32)
    pre_low = probs_low[..., :PREFIX_TOKENS]
    own_low = probs_low[..., PREFIX_TOKENS:]
    attended = jnp.einsum('hgsp,phd->shgd', pre_low, values_wide) + jnp.einsum('hgst,thd->shgd', own_low, sequence_values.astype(jnp.float32))
    active_rows = (jnp.arange(sequence_rows) < length)[:, None, None, None]
    attention_out = jnp.where(active_rows, attended, 0.0).astype(jnp.bfloat16)
    upstream_gradient = jnp.where(active_rows, upstream_unshaped.reshape(sequence_rows, KEY_VALUE_HEADS, query_group_size, HEAD_SIZE), 0.0).astype(jnp.bfloat16)
    upstream_wide = upstream_gradient.astype(jnp.float32)
    delta = jnp.einsum('shgd,shgd->hgs', upstream_wide, attention_out.astype(jnp.float32))
    dprob = jnp.einsum('shgd,phd->hgsp', upstream_wide, values_wide)
    dscore = (pre_probs * (dprob - delta[..., None])).astype(jnp.bfloat16).astype(jnp.float32)
    gradient_keys = jnp.einsum('hgsp,shgd->phd', dscore, grouped_heads) * score_scale
    gradient_values = jnp.einsum('hgsp,shgd->phd', pre_low, upstream_wide)
    conversation_term = jnp.concatenate([gradient_keys.reshape(PREFIX_TOKENS, KEY_VALUE_HEADS * HEAD_SIZE), gradient_values.reshape(PREFIX_TOKENS, KEY_VALUE_HEADS * HEAD_SIZE)], axis=1)
    return (attention_out.reshape(sequence_rows, QUERY_HEADS * HEAD_SIZE), conversation_term)

def reference(hidden, norm_gain, query_weight, key_value_weight, lengths, cotangent, cartridge, adam_first_moment, adam_second_moment):
    cartridge_prefix = cartridge.astype(jnp.bfloat16)
    cartridge_keys = cartridge_prefix[:, :KEY_VALUE_HEADS * HEAD_SIZE].reshape(PREFIX_TOKENS, KEY_VALUE_HEADS, HEAD_SIZE)
    cartridge_values = cartridge_prefix[:, KEY_VALUE_HEADS * HEAD_SIZE:].reshape(PREFIX_TOKENS, KEY_VALUE_HEADS, HEAD_SIZE)

    def accumulate_rows(running, inputs):
        states, length, upstream_unshaped = inputs
        attended, conversation_term = one_conversation(states, length, upstream_unshaped, cartridge_keys, cartridge_values, query_weight, key_value_weight, norm_gain)
        return (running + conversation_term, attended)
    prefix_gradient, layer_outputs = lax.scan(accumulate_rows, jnp.zeros((PREFIX_TOKENS, 2 * KEY_VALUE_HEADS * HEAD_SIZE), jnp.float32), (hidden, lengths, cotangent))
    new_cartridge, new_first, new_second = adam_update(cartridge, adam_first_moment, adam_second_moment, prefix_gradient)
    return (layer_outputs, new_cartridge, new_first, new_second)
```

```python
import jax
import jax.numpy as jnp
from jax import lax
from jax.experimental import pallas as pl
from jax.experimental.pallas import tpu as pltpu
from jax.sharding import PartitionSpec as P

HEAD_SIZE = 128
GROUP = 4
STEP = 50
ROWS = 256
WIDTH = 4096
PREFIX = 512
COLS = 768
HALF = 384
MESH_AXES = ("fsdp", "dp", "owner")
X_SIZE, Z_SIZE = 4, 8
LOG2E = 1.4426950408889634


def coords(i):
    return i // 128, (i % 128) // 32, (i // 4) % 8, (i // 2) % 2, i % 2


def device_at(y_hi, x, z, y_lo, core):
    return y_hi * 128 + (x * 8 + z) * 4 + y_lo * 2 + core


def permute(value, move):
    pairs = [(i, device_at(*move(*coords(i)))) for i in range(256)]
    return lax.ppermute(value, MESH_AXES, pairs)


def along_z(step):
    return lambda y_hi, x, z, y_lo, core: (y_hi, x, (z + step) % Z_SIZE, y_lo, core)


def along_x(step):
    return lambda y_hi, x, z, y_lo, core: (y_hi, (x + step) % X_SIZE, z, y_lo, core)


def other_core(y_hi, x, z, y_lo, core):
    return y_hi, x, z, y_lo, 1 - core


def pair_chip(y_hi, x, z, y_lo, core):
    return y_hi, x, z, 1 - y_lo, core


def across_y(y_hi, x, z, y_lo, core):
    return 1 - y_hi, x, z, 1 - y_lo, core


X_GROUPS = [[x * Z_SIZE + z for x in range(X_SIZE)] for z in range(Z_SIZE)]
Z_GROUPS = [[x * Z_SIZE + z for z in range(Z_SIZE)] for x in range(X_SIZE)]


def spread(value, axes, members, groups=None):
    copies = jnp.broadcast_to(value[None], (members,) + value.shape)
    return lax.all_to_all(copies, axes, 0, 0, axis_index_groups=groups, tiled=True)


def rope_tables():
    exponent = jnp.arange(HEAD_SIZE // 2, dtype=jnp.float32) * (2.0 / HEAD_SIZE)
    inverse = jnp.power(jnp.float32(500000.0), -exponent)
    position = (PREFIX + jnp.arange(ROWS)).astype(jnp.float32)
    angles = position[:, None] * inverse[None, :]
    cosine, sine = jnp.cos(angles), jnp.sin(angles)
    return (
        jnp.concatenate([cosine, cosine], axis=1),
        jnp.concatenate([-sine, sine], axis=1),
    )


def dot(a, b, a_dim, b_dim):
    return lax.dot_general(
        a, b, (((a_dim,), (b_dim,)), ((), ())), preferred_element_type=jnp.float32
    )


def norm_kernel(states, gain, normed):
    wide = states[0].astype(jnp.float32)
    scale = lax.rsqrt(jnp.mean(wide * wide, axis=1, keepdims=True) + 1e-05)
    normed[...] = (wide * scale * gain[...]).astype(jnp.bfloat16)


def normalise(hidden, gain):
    return pl.pallas_call(
        norm_kernel,
        grid=(4,),
        in_specs=[
            pl.BlockSpec((1, 64, WIDTH), lambda i: (0, i, 0)),
            pl.BlockSpec((1, WIDTH), lambda i: (0, 0)),
        ],
        out_specs=pl.BlockSpec((64, WIDTH), lambda i: (i, 0)),
        out_shape=jax.ShapeDtypeStruct((ROWS, WIDTH), jnp.bfloat16),
    )(hidden, gain.reshape(1, WIDTH))


def live(length):
    return lax.broadcasted_iota(jnp.int32, (ROWS, 512), 0) < length


def pack_kernel(lengths, cotangent, key_rows, value_rows, packed):
    packed[0, 0:ROWS, :] = jnp.where(live(lengths[0]), cotangent[0], 0).astype(jnp.bfloat16)
    for half in range(2):
        rows = slice(half * 64, half * 64 + 64)
        packed[0, ROWS:, half * 128 : half * 128 + 128] = key_rows[rows, :].astype(jnp.bfloat16)
        packed[0, ROWS:, 256 + half * 128 : 384 + half * 128] = value_rows[rows, :].astype(
            jnp.bfloat16
        )


def pack(lengths, cotangent, cartridge):
    return pl.pallas_call(
        pack_kernel,
        grid_spec=pltpu.PrefetchScalarGridSpec(
            num_scalar_prefetch=1,
            grid=(4,),
            in_specs=[
                pl.BlockSpec((1, ROWS, 512), lambda i, n: (0, 0, i)),
                pl.BlockSpec((128, 128), lambda i, n: (0, i)),
                pl.BlockSpec((128, 128), lambda i, n: (0, 4 + i)),
            ],
            out_specs=pl.BlockSpec((1, 320, 512), lambda i, n: (i, 0, 0)),
        ),
        out_shape=jax.ShapeDtypeStruct((4, 320, 512), jnp.bfloat16),
    )(lengths, cotangent, cartridge, cartridge)


def unpack_kernel(lengths, attended, out):
    out[0] = jnp.where(live(lengths[0]), attended[0], 0).astype(jnp.bfloat16)


def unpack(lengths, attended):
    return pl.pallas_call(
        unpack_kernel,
        grid_spec=pltpu.PrefetchScalarGridSpec(
            num_scalar_prefetch=1,
            grid=(4,),
            in_specs=[pl.BlockSpec((1, ROWS, 512), lambda i, n: (i, 0, 0))],
            out_specs=pl.BlockSpec((1, ROWS, 512), lambda i, n: (0, 0, i)),
        ),
        out_shape=jax.ShapeDtypeStruct((1, ROWS, 2048), jnp.bfloat16),
    )(lengths, attended)


def layer_kernel(place, *refs):
    states = refs[0:4]
    z_pieces = refs[4:13]
    x_pieces = refs[13:18]
    packed, cosine, sine = refs[18:21]
    out, gradient = refs[21:23]
    weights, rows, keys, values, sums, piece_sem, row_sem = refs[23:]
    step = pl.program_id(0)
    y_hi, x, z = place[1], place[2], place[3]

    def piece_copies():
        copies = []

        def add(source, target):
            copies.append(
                pltpu.make_async_copy(source, target, piece_sem.at[len(copies)])
            )

        offsets = (0, -1, 1, -2, 2, -3, 3)
        for side in range(2):
            y_from = y_hi if side == 0 else 1 - y_hi
            part = pl.ds(side * 64, 64)
            for piece, offset in zip(z_pieces[:7], offsets):
                z_from = lax.rem(z + (offset + Z_SIZE), Z_SIZE)
                add(
                    piece.at[:, part, :],
                    weights.at[y_from, :, z_from, :, pl.ds(0, HALF)],
                )
            z_from = lax.rem(z + 4, Z_SIZE)
            add(
                z_pieces[7].at[:, part, :],
                weights.at[y_from, pl.ds(0, 2), z_from, :, pl.ds(0, HALF)],
            )
            add(
                z_pieces[8].at[:, part, :],
                weights.at[y_from, pl.ds(2, 2), z_from, :, pl.ds(0, HALF)],
            )
            for piece, offset in zip(x_pieces[:3], (0, -1, 1)):
                x_from = lax.rem(x + (offset + X_SIZE), X_SIZE)
                add(
                    piece.at[:, part, :],
                    weights.at[y_from, x_from, :, :, pl.ds(HALF, HALF)],
                )
            x_from = lax.rem(x + 2, X_SIZE)
            add(
                x_pieces[3].at[:, part, :],
                weights.at[y_from, x_from, pl.ds(0, 4), :, pl.ds(HALF, HALF)],
            )
            add(
                x_pieces[4].at[:, part, :],
                weights.at[y_from, x_from, pl.ds(4, 4), :, pl.ds(HALF, HALF)],
            )
        return copies

    def row_copy(index):
        slot = index % 2
        return pltpu.make_async_copy(states[index], rows.at[slot], row_sem.at[slot])

    @pl.when(step == 0)
    def _():
        for copy in piece_copies():
            copy.start()
        row_copy(0).start()
        row_copy(1).start()
        for owner in range(4):
            base = pl.ds(owner * 128, 64)
            tail = pl.ds(owner * 128 + 64, 64)
            keys[base, :] = packed[owner, 256:320, 0:128]
            keys[tail, :] = packed[owner, 256:320, 128:256]
            values[base, :] = packed[owner, 256:320, 256:384]
            values[tail, :] = packed[owner, 256:320, 384:512]
        sums[...] = jnp.zeros_like(sums)
        for copy in piece_copies():
            copy.wait()

    for index in range(4):

        @pl.when(step == index)
        def _():
            if index in (1, 2):
                row_copy(index + 1).start()
            row_copy(index).wait()

    slot = lax.rem(step, 2)
    conversation = place[0] ^ step
    projected = dot(rows[slot], weights[...].reshape(WIDTH, COLS), 1, 0)
    cos, sin = cosine[...], sine[...]

    def rope(v):
        return (v * cos + pltpu.roll(v, HEAD_SIZE // 2, 1) * sin).astype(jnp.bfloat16)

    own_keys = rope(projected[:, 512:640])
    own_values = projected[:, 640:768].astype(jnp.bfloat16)
    prefix_keys, prefix_values = keys[...], values[...]
    causal = lax.broadcasted_iota(jnp.int32, (ROWS, ROWS), 0) >= lax.broadcasted_iota(
        jnp.int32, (ROWS, ROWS), 1
    )
    scale = HEAD_SIZE ** (-0.5) * LOG2E
    key_sum = jnp.zeros((HEAD_SIZE, PREFIX), jnp.float32)
    value_sum = jnp.zeros((HEAD_SIZE, PREFIX), jnp.float32)
    for head in range(GROUP):
        lanes = slice(head * HEAD_SIZE, (head + 1) * HEAD_SIZE)
        query = rope(projected[:, lanes])
        upstream = packed[conversation, 0:ROWS, lanes]
        before = dot(query, prefix_keys, 1, 1) * scale
        own = jnp.where(causal, dot(query, own_keys, 1, 1) * scale, -1e30)
        highest = jnp.maximum(
            jnp.max(before, axis=1, keepdims=True), jnp.max(own, axis=1, keepdims=True)
        )
        before = jnp.exp2(before - highest)
        own = jnp.exp2(own - highest)
        total = jnp.sum(before, axis=1, keepdims=True) + jnp.sum(own, axis=1, keepdims=True)
        inverse = 1.0 / total
        probs = before * inverse
        probs_low = probs.astype(jnp.bfloat16)
        own_low = (own * inverse).astype(jnp.bfloat16)
        attended = (
            dot(probs_low, prefix_values, 1, 0) + dot(own_low, own_values, 1, 0)
        ).astype(jnp.bfloat16)
        out[0, :, lanes] = attended
        delta = jnp.sum(
            upstream.astype(jnp.float32) * attended.astype(jnp.float32),
            axis=1,
            keepdims=True,
        )
        dprob = dot(upstream, prefix_values, 1, 1)
        dscore = (probs * (dprob - delta)).astype(jnp.bfloat16)
        key_sum += dot(query, dscore, 0, 0)
        value_sum += dot(upstream, probs_low, 0, 0)
    sums[0:HEAD_SIZE, :] += key_sum * HEAD_SIZE ** (-0.5)
    sums[HEAD_SIZE:, :] += value_sum

    @pl.when(step == 3)
    def _():
        gradient[...] = sums[...].T.astype(gradient.dtype)


def layer(place, states, z_pieces, x_pieces, packed, cosine, sine):
    anywhere = pl.BlockSpec(memory_space=pl.ANY)

    def whole(shape):
        return pl.BlockSpec(
            shape, lambda i, place: (0,) * len(shape), pipeline_mode=pl.Buffered(1)
        )

    return pl.pallas_call(
        layer_kernel,
        grid_spec=pltpu.PrefetchScalarGridSpec(
            num_scalar_prefetch=1,
            grid=(4,),
            in_specs=[anywhere] * 18
            + [whole(packed.shape), whole(cosine.shape), whole(sine.shape)],
            out_specs=[
                pl.BlockSpec((1, ROWS, 512), lambda i, place: (place[0] ^ i, 0, 0)),
                pl.BlockSpec((PREFIX, 256), lambda i, place: (0, 0)),
            ],
            scratch_shapes=[
                pltpu.VMEM((2, X_SIZE, Z_SIZE, 64, COLS), jnp.bfloat16),
                pltpu.VMEM((2, ROWS, WIDTH), jnp.bfloat16),
                pltpu.VMEM((PREFIX, HEAD_SIZE), jnp.bfloat16),
                pltpu.VMEM((PREFIX, HEAD_SIZE), jnp.bfloat16),
                pltpu.VMEM((256, PREFIX), jnp.float32),
                pltpu.SemaphoreType.DMA((28,)),
                pltpu.SemaphoreType.DMA((2,)),
            ],
        ),
        out_shape=[
            jax.ShapeDtypeStruct((4, ROWS, 512), jnp.bfloat16),
            jax.ShapeDtypeStruct((PREFIX, 256), jnp.bfloat16),
        ],
        compiler_params=pltpu.CompilerParams(dimension_semantics=("arbitrary",)),
    )(place, *states, *z_pieces, *x_pieces, packed, cosine, sine)


def gather_weights(query_weight, key_value_weight, head):
    def of_head(index):
        return jnp.concatenate(
            [
                lax.dynamic_slice_in_dim(query_weight, index * 512, 512, 1),
                lax.dynamic_slice_in_dim(key_value_weight, index * 128, 128, 1),
                lax.dynamic_slice_in_dim(key_value_weight, 512 + index * 128, 128, 1),
            ],
            axis=1,
        )

    both = jnp.concatenate([of_head(head), permute(of_head(head ^ 2), across_y)], axis=0)
    first = spread(both[:, :HALF], "dp", X_SIZE, X_GROUPS)
    second = spread(both[:, HALF:], "dp", Z_SIZE, Z_GROUPS)
    z_pieces = [first]
    up, down = first, first
    for _ in range(3):
        up, down = permute(up, along_z(1)), permute(down, along_z(-1))
        z_pieces += [up, down]
    z_pieces += [permute(up[:2], along_z(1)), permute(down[2:], along_z(-1))]
    up, down = permute(second, along_x(1)), permute(second, along_x(-1))
    x_pieces = [second, up, down]
    x_pieces += [permute(up[:4], along_x(1)), permute(down[4:], along_x(-1))]
    return z_pieces, x_pieces


def adam_update(current, moment_one, moment_two, prefix_gradient):
    one_new = 0.9 * moment_one + 0.1 * prefix_gradient
    two_new = 0.999 * moment_two + 0.001 * prefix_gradient * prefix_gradient
    one_fix = 1.0 - 0.9**STEP
    two_fix = 1.0 - 0.999**STEP
    updated = current - 0.02 * (one_new / one_fix) / (jnp.sqrt(two_new / two_fix) + 1e-08)
    return (updated, one_new, two_new)


def on_device(
    hidden,
    norm_gain,
    query_weight,
    key_value_weight,
    lengths,
    cotangent,
    cartridge,
    adam_first_moment,
    adam_second_moment,
):
    head = lax.axis_index("owner")
    replica = lax.axis_index("dp")
    z_pieces, x_pieces = gather_weights(query_weight, key_value_weight, head)

    normed = normalise(hidden, norm_gain)
    near = permute(normed, other_core)
    far = permute(normed, pair_chip)
    farthest = permute(far, other_core)

    packed = lax.all_to_all(pack(lengths, cotangent, cartridge), "owner", 0, 0, tiled=True)
    cosine, sine = rope_tables()
    place = jnp.stack(
        [head, lax.axis_index("fsdp"), replica // Z_SIZE, replica % Z_SIZE]
    ).astype(jnp.int32)
    attended, gradient = layer(
        place, (normed, near, far, farthest), z_pieces, x_pieces, packed, cosine, sine
    )

    terms = lax.all_to_all(
        gradient.reshape(256, 2, 256), ("owner", "fsdp", "dp"), 0, 0, tiled=True
    )
    summed = jnp.sum(terms.reshape(4, 64, 2, 2, 128).astype(jnp.float32), axis=1)
    summed = summed.transpose(1, 2, 0, 3).reshape(2, 1024)
    owned = spread(summed.astype(jnp.bfloat16), ("fsdp", "dp"), 64)
    owned = owned.reshape(128, 1024).astype(jnp.float32)

    returned = lax.all_to_all(attended, "owner", 0, 0, tiled=True)
    attention_out = unpack(lengths, returned)
    new_cartridge, new_first, new_second = adam_update(
        cartridge, adam_first_moment, adam_second_moment, owned
    )
    return attention_out, new_cartridge, new_first, new_second


def solution(mesh):
    placed = (
        P(MESH_AXES, None, None),
        P(),
        P(("fsdp", "dp"), None),
        P(("fsdp", "dp"), None),
        P(MESH_AXES),
        P(MESH_AXES, None, None),
        P("owner", None),
        P("owner", None),
        P("owner", None),
    )
    return jax.shard_map(
        on_device,
        mesh=mesh,
        in_specs=placed,
        out_specs=(
            P(MESH_AXES, None, None),
            P("owner", None),
            P("owner", None),
            P("owner", None),
        ),
        check_vma=False,
    )
```

```python
import jax
import jax.numpy as jnp
from jax import lax
from jax.experimental import pallas as pl
from jax.experimental.pallas import tpu as pltpu
from jax.sharding import PartitionSpec as P


HEAD_SIZE = 128
GROUP = 4
STEP = 50
ROWS = 256
WIDTH = 4096
PREFIX = 512
COLS = 768
HALF = 384
MESH_AXES = ("fsdp", "dp", "owner")
X_SIZE, Z_SIZE = 4, 8
LOG2E = 1.4426950408889634


def coords(i):
    return i // 128, (i % 128) // 32, (i // 4) % 8, (i // 2) % 2, i % 2


def device_at(y_hi, x, z, y_lo, core):
    return y_hi * 128 + (x * 8 + z) * 4 + y_lo * 2 + core


def permute(value, move):
    pairs = [(i, device_at(*move(*coords(i)))) for i in range(256)]
    return lax.ppermute(value, MESH_AXES, pairs)


def along_z(step):
    return lambda y_hi, x, z, y_lo, core: (y_hi, x, (z + step) % Z_SIZE, y_lo, core)


def along_x(step):
    return lambda y_hi, x, z, y_lo, core: (y_hi, (x + step) % X_SIZE, z, y_lo, core)


def other_core(y_hi, x, z, y_lo, core):
    return y_hi, x, z, y_lo, 1 - core


def pair_chip(y_hi, x, z, y_lo, core):
    return y_hi, x, z, 1 - y_lo, core


def across_y(y_hi, x, z, y_lo, core):
    return 1 - y_hi, x, z, 1 - y_lo, core


def other_pair(y_hi, x, z, y_lo, core):
    return y_hi, x, z, 1 - y_lo, 1 - core


OWNERS = (other_core, pair_chip, other_pair)
Z_GROUPS = [[x * Z_SIZE + z for z in range(Z_SIZE)] for x in range(X_SIZE)]


def spread(value, axes, members, groups=None):
    copies = jnp.broadcast_to(value[None], (members,) + value.shape)
    return lax.all_to_all(copies, axes, 0, 0, axis_index_groups=groups, tiled=True)


def rope_tables():
    exponent = jnp.arange(HEAD_SIZE // 2, dtype=jnp.float32) * (2.0 / HEAD_SIZE)
    inverse = jnp.power(jnp.float32(500000.0), -exponent)
    position = (PREFIX + jnp.arange(ROWS)).astype(jnp.float32)
    angles = position[:, None] * inverse[None, :]
    cosine, sine = jnp.cos(angles), jnp.sin(angles)
    return (
        jnp.concatenate([cosine, cosine], axis=1),
        jnp.concatenate([-sine, sine], axis=1),
    )


def dot(a, b, a_dim, b_dim):
    return lax.dot_general(
        a, b, (((a_dim,), (b_dim,)), ((), ())), preferred_element_type=jnp.float32
    )


def norm_kernel(states, gain, normed):
    wide = states[0].astype(jnp.float32)
    scale = lax.rsqrt(jnp.mean(wide * wide, axis=1, keepdims=True) + 1e-05)
    normed[...] = (wide * scale * gain[...]).astype(jnp.bfloat16)


def normalise(hidden, gain):
    return pl.pallas_call(
        norm_kernel,
        grid=(4,),
        in_specs=[
            pl.BlockSpec((1, 64, WIDTH), lambda i: (0, i, 0)),
            pl.BlockSpec((1, WIDTH), lambda i: (0, 0)),
        ],
        out_specs=pl.BlockSpec((64, WIDTH), lambda i: (i, 0)),
        out_shape=jax.ShapeDtypeStruct((ROWS, WIDTH), jnp.bfloat16),
    )(hidden, gain.reshape(1, WIDTH))


def live(length):
    return lax.broadcasted_iota(jnp.int32, (ROWS, 512), 0) < length


def pack_kernel(place, cotangent, key_rows, value_rows, *packed):
    for index in range(4):

        @pl.when(pl.program_id(0) == index)
        def _():
            target = packed[index]
            target[0:ROWS, :] = jnp.where(live(place[4]), cotangent[0], 0).astype(jnp.bfloat16)
            for half in range(2):
                rows = slice(half * 64, half * 64 + 64)
                target[ROWS:, half * 128 : half * 128 + 128] = key_rows[rows, :].astype(
                    jnp.bfloat16
                )
                target[ROWS:, 256 + half * 128 : 384 + half * 128] = value_rows[rows, :].astype(
                    jnp.bfloat16
                )


def pack(place, cotangent, cartridge):
    return pl.pallas_call(
        pack_kernel,
        grid_spec=pltpu.PrefetchScalarGridSpec(
            num_scalar_prefetch=1,
            grid=(4,),
            in_specs=[
                pl.BlockSpec((1, ROWS, 512), lambda i, place: (0, 0, place[0] ^ i)),
                pl.BlockSpec((128, 128), lambda i, place: (0, place[0] ^ i)),
                pl.BlockSpec((128, 128), lambda i, place: (0, 4 + (place[0] ^ i))),
            ],
            out_specs=[pl.BlockSpec((320, 512), lambda i, place: (0, 0))] * 4,
        ),
        out_shape=[jax.ShapeDtypeStruct((320, 512), jnp.bfloat16)] * 4,
    )(place, cotangent, cartridge, cartridge)


def unpack_kernel(place, *refs):
    out = refs[4]
    for index in range(4):

        @pl.when(pl.program_id(0) == index)
        def _():
            out[0] = jnp.where(live(place[4]), refs[index][...], 0).astype(jnp.bfloat16)


def unpack(place, pieces):
    return pl.pallas_call(
        unpack_kernel,
        grid_spec=pltpu.PrefetchScalarGridSpec(
            num_scalar_prefetch=1,
            grid=(4,),
            in_specs=[pl.BlockSpec((ROWS, 512), lambda i, place: (0, 0))] * 4,
            out_specs=pl.BlockSpec((1, ROWS, 512), lambda i, place: (0, 0, place[0] ^ i)),
        ),
        out_shape=jax.ShapeDtypeStruct((1, ROWS, 2048), jnp.bfloat16),
    )(place, *pieces)


def layer_kernel(place, *refs):
    states = refs[0:4]
    z_pieces = refs[4:12]
    x_pieces = refs[12:17]
    packed, cosine, sine = refs[17:21], refs[21], refs[22]
    outs, gradient = refs[23:27], refs[27]
    weights, rows, keys, values, ups, out, sums, piece_sem, row_sem, up_sem = refs[28:]
    step = pl.program_id(0)
    y_hi, x, z = place[1], place[2], place[3]

    def piece_copies():
        copies = []

        def add(source, target):
            copies.append(
                pltpu.make_async_copy(source, target, piece_sem.at[len(copies)])
            )

        offsets = (0, -1, 1, -2, 2, -3, 3, 4)
        for side in range(2):
            y_from = y_hi if side == 0 else 1 - y_hi
            part = pl.ds(side * 64, 64)
            for piece, offset in zip(z_pieces, offsets):
                z_from = lax.rem(z + (offset + Z_SIZE), Z_SIZE)
                for back in range(X_SIZE):
                    x_from = lax.rem(x + (X_SIZE - back), X_SIZE)
                    add(
                        piece.at[back, part, :],
                        weights.at[y_from, x_from, z_from, :, pl.ds(0, HALF)],
                    )
            for piece, offset in zip(x_pieces[:3], (0, -1, 1)):
                x_from = lax.rem(x + (offset + X_SIZE), X_SIZE)
                add(
                    piece.at[:, part, :],
                    weights.at[y_from, x_from, :, :, pl.ds(HALF, HALF)],
                )
            x_from = lax.rem(x + 2, X_SIZE)
            add(
                x_pieces[3].at[:, part, :],
                weights.at[y_from, x_from, pl.ds(0, 4), :, pl.ds(HALF, HALF)],
            )
            add(
                x_pieces[4].at[:, part, :],
                weights.at[y_from, x_from, pl.ds(4, 4), :, pl.ds(HALF, HALF)],
            )
        return copies

    def row_copy(index):
        slot = index % 2
        return pltpu.make_async_copy(states[index], rows.at[slot], row_sem.at[slot])

    def up_copies():
        return [
            pltpu.make_async_copy(packed[index], ups.at[index], up_sem.at[index])
            for index in range(4)
        ]

    @pl.when(step == 0)
    def _():
        for copy in piece_copies():
            copy.start()
        row_copy(0).start()
        row_copy(1).start()
        for copy in up_copies():
            copy.start()
        sums[...] = jnp.zeros_like(sums)
        for copy in up_copies():
            copy.wait()
        for index in range(4):
            first = pl.multiple_of((place[0] ^ index) * 128, 128)
            for half in range(2):
                target = pl.ds(first + half * 64, 64)
                keys[target, :] = ups[index, ROWS:, half * 128 : half * 128 + 128]
                values[target, :] = ups[index, ROWS:, 256 + half * 128 : 384 + half * 128]
        for copy in piece_copies():
            copy.wait()

    for index in range(4):

        @pl.when(step == index)
        def _():
            if index in (1, 2):
                row_copy(index + 1).start()
            row_copy(index).wait()

    slot = lax.rem(step, 2)
    projected = dot(rows[slot], weights[...].reshape(WIDTH, COLS), 1, 0)
    cos, sin = cosine[...], sine[...]

    def rope(v):
        return (v * cos + pltpu.roll(v, HEAD_SIZE // 2, 1) * sin).astype(jnp.bfloat16)

    own_keys = rope(projected[:, 512:640])
    own_values = projected[:, 640:768].astype(jnp.bfloat16)
    prefix_keys, prefix_values = keys[...], values[...]
    causal = lax.broadcasted_iota(jnp.int32, (ROWS, ROWS), 0) >= lax.broadcasted_iota(
        jnp.int32, (ROWS, ROWS), 1
    )
    scale = HEAD_SIZE ** (-0.5) * LOG2E
    key_sum = jnp.zeros((HEAD_SIZE, PREFIX), jnp.float32)
    value_sum = jnp.zeros((HEAD_SIZE, PREFIX), jnp.float32)
    for head in range(GROUP):
        lanes = slice(head * HEAD_SIZE, (head + 1) * HEAD_SIZE)
        query = rope(projected[:, lanes])
        upstream = ups[step, 0:ROWS, lanes]
        before = dot(query, prefix_keys, 1, 1) * scale
        own = jnp.where(causal, dot(query, own_keys, 1, 1) * scale, -1e30)
        highest = jnp.maximum(
            jnp.max(before, axis=1, keepdims=True), jnp.max(own, axis=1, keepdims=True)
        )
        before = jnp.exp2(before - highest)
        own = jnp.exp2(own - highest)
        total = jnp.sum(before, axis=1, keepdims=True) + jnp.sum(own, axis=1, keepdims=True)
        inverse = 1.0 / total
        probs = before * inverse
        probs_low = probs.astype(jnp.bfloat16)
        own_low = (own * inverse).astype(jnp.bfloat16)
        attended = (
            dot(probs_low, prefix_values, 1, 0) + dot(own_low, own_values, 1, 0)
        ).astype(jnp.bfloat16)
        out[:, lanes] = attended
        delta = jnp.sum(
            upstream.astype(jnp.float32) * attended.astype(jnp.float32),
            axis=1,
            keepdims=True,
        )
        dprob = dot(upstream, prefix_values, 1, 1)
        dscore = (probs * (dprob - delta)).astype(jnp.bfloat16)
        key_sum += dot(query, dscore, 0, 0)
        value_sum += dot(upstream, probs_low, 0, 0)
    sums[0:HEAD_SIZE, :] += key_sum * HEAD_SIZE ** (-0.5)
    sums[HEAD_SIZE:, :] += value_sum

    for index in range(4):

        @pl.when(step == index)
        def _():
            outs[index][...] = out[...]

    @pl.when(step == 3)
    def _():
        gradient[...] = sums[...].T.astype(gradient.dtype)


def layer(place, states, z_pieces, x_pieces, packed, cosine, sine):
    anywhere = pl.BlockSpec(memory_space=pl.ANY)

    def whole(shape):
        return pl.BlockSpec(
            shape, lambda i, place: (0,) * len(shape), pipeline_mode=pl.Buffered(1)
        )

    return pl.pallas_call(
        layer_kernel,
        grid_spec=pltpu.PrefetchScalarGridSpec(
            num_scalar_prefetch=1,
            grid=(4,),
            in_specs=[anywhere] * 21 + [whole(cosine.shape), whole(sine.shape)],
            out_specs=[pl.BlockSpec((ROWS, 512), lambda i, place: (0, 0))] * 4
            + [
                pl.BlockSpec((PREFIX, 256), lambda i, place: (0, 0)),
            ],
            scratch_shapes=[
                pltpu.VMEM((2, X_SIZE, Z_SIZE, 64, COLS), jnp.bfloat16),
                pltpu.VMEM((2, ROWS, WIDTH), jnp.bfloat16),
                pltpu.VMEM((PREFIX, HEAD_SIZE), jnp.bfloat16),
                pltpu.VMEM((PREFIX, HEAD_SIZE), jnp.bfloat16),
                pltpu.VMEM((4, 320, 512), jnp.bfloat16),
                pltpu.VMEM((ROWS, 512), jnp.bfloat16),
                pltpu.VMEM((256, PREFIX), jnp.float32),
                pltpu.SemaphoreType.DMA((74,)),
                pltpu.SemaphoreType.DMA((2,)),
                pltpu.SemaphoreType.DMA((4,)),
            ],
        ),
        out_shape=[jax.ShapeDtypeStruct((ROWS, 512), jnp.bfloat16)] * 4
        + [
            jax.ShapeDtypeStruct((PREFIX, 256), jnp.bfloat16),
        ],
        compiler_params=pltpu.CompilerParams(dimension_semantics=("arbitrary",)),
    )(place, *states, *z_pieces, *x_pieces, *packed, cosine, sine)


def of_head(query_weight, key_value_weight, index):
    return jnp.concatenate(
        [
            lax.dynamic_slice_in_dim(query_weight, index * 512, 512, 1),
            lax.dynamic_slice_in_dim(key_value_weight, index * 128, 128, 1),
            lax.dynamic_slice_in_dim(key_value_weight, 512 + index * 128, 128, 1),
        ],
        axis=1,
    )


def gather_weights(own, across):
    both = jnp.concatenate([own, across], axis=0)
    first = both[:, :HALF]
    first = jnp.stack([first] + [permute(first, along_x(step)) for step in (1, 2, 3)])
    second = spread(both[:, HALF:], "dp", Z_SIZE, Z_GROUPS)
    z_pieces = [first]
    up, down = first, first
    for _ in range(3):
        up, down = permute(up, along_z(1)), permute(down, along_z(-1))
        z_pieces += [up, down]
    z_pieces += [permute(up, along_z(1))]
    up, down = permute(second, along_x(1)), permute(second, along_x(-1))
    x_pieces = [second, up, down]
    x_pieces += [permute(up[:4], along_x(1)), permute(down[4:], along_x(-1))]
    return z_pieces, x_pieces


def adam_update(current, moment_one, moment_two, prefix_gradient):
    one_new = 0.9 * moment_one + 0.1 * prefix_gradient
    two_new = 0.999 * moment_two + 0.001 * prefix_gradient * prefix_gradient
    one_fix = 1.0 - 0.9**STEP
    two_fix = 1.0 - 0.999**STEP
    updated = current - 0.02 * (one_new / one_fix) / (jnp.sqrt(two_new / two_fix) + 1e-08)
    return (updated, one_new, two_new)


def layer_step(
    hidden,
    norm_gain,
    query_weight,
    key_value_weight,
    lengths,
    cotangent,
    cartridge,
    adam_first_moment,
    adam_second_moment,
):
    head = lax.axis_index("owner")
    replica = lax.axis_index("dp")
    cosine, sine = rope_tables()
    place = jnp.stack(
        [head, lax.axis_index("fsdp"), replica // Z_SIZE, replica % Z_SIZE, lengths[0]]
    ).astype(jnp.int32)
    sent = of_head(query_weight, key_value_weight, head ^ 2)
    own = of_head(query_weight, key_value_weight, head)
    own, sent, hidden = lax.optimization_barrier((own, sent, hidden))
    across = permute(sent, across_y)
    normed = normalise(hidden, norm_gain)
    far = permute(normed, pair_chip)
    near = permute(normed, other_core)
    packed = pack(place, cotangent, cartridge)
    across, packed, cosine, sine = lax.optimization_barrier((across, packed, cosine, sine))
    z_pieces, x_pieces = gather_weights(own, across)
    packed = [packed[0]] + [permute(v, m) for v, m in zip(packed[1:], OWNERS)]
    far, z_pieces[5], z_pieces[6] = lax.optimization_barrier((far, z_pieces[5], z_pieces[6]))
    farthest = permute(far, other_core)
    *attended, gradient = layer(
        place, (normed, near, far, farthest), z_pieces, x_pieces, packed, cosine, sine
    )

    returned = [attended[0]] + [permute(v, m) for v, m in zip(attended[1:], OWNERS)]
    terms = lax.all_to_all(gradient.reshape(256, 2, 256), ("owner", "fsdp", "dp"), 0, 0, tiled=True)
    summed = jnp.sum(terms.reshape(4, 64, 2, 2, 128).astype(jnp.float32), axis=1)
    summed = summed.transpose(1, 2, 0, 3).reshape(2, 1024)
    owned = spread(summed.astype(jnp.bfloat16), ("fsdp", "dp"), 64)
    owned = owned.reshape(128, 1024).astype(jnp.float32)
    attention_out = unpack(place, returned)
    new_cartridge, new_first, new_second = adam_update(
        cartridge, adam_first_moment, adam_second_moment, owned
    )
    return attention_out, new_cartridge, new_first, new_second


def solution(mesh):
    placed = (
        P(MESH_AXES, None, None),
        P(),
        P(("fsdp", "dp"), None),
        P(("fsdp", "dp"), None),
        P(MESH_AXES),
        P(MESH_AXES, None, None),
        P("owner", None),
        P("owner", None),
        P("owner", None),
    )
    return jax.shard_map(
        layer_step,
        mesh=mesh,
        in_specs=placed,
        out_specs=(
            P(MESH_AXES, None, None),
            P("owner", None),
            P("owner", None),
            P("owner", None),
        ),
        check_vma=False,
    )
```

```python
import jax
import jax.numpy as jnp
from jax import lax
from jax.experimental import pallas as pl
from jax.experimental.pallas import tpu as pltpu
from jax.sharding import PartitionSpec as P


HEAD_SIZE = 128
GROUP = 4
STEP = 50
ROWS = 256
WIDTH = 4096
PREFIX = 512
COLS = 768
HALF = 384
MESH_AXES = ("fsdp", "dp", "owner")
X_SIZE, Z_SIZE = 4, 8
LOG2E = 1.4426950408889634


def coords(i):
    return i // 128, (i % 128) // 32, (i // 4) % 8, (i // 2) % 2, i % 2


def device_at(y_hi, x, z, y_lo, core):
    return y_hi * 128 + (x * 8 + z) * 4 + y_lo * 2 + core


def permute(value, move):
    pairs = [(i, device_at(*move(*coords(i)))) for i in range(256)]
    return lax.ppermute(value, MESH_AXES, pairs)


def along_z(step):
    return lambda y_hi, x, z, y_lo, core: (y_hi, x, (z + step) % Z_SIZE, y_lo, core)


def along_x(step):
    return lambda y_hi, x, z, y_lo, core: (y_hi, (x + step) % X_SIZE, z, y_lo, core)


def other_core(y_hi, x, z, y_lo, core):
    return y_hi, x, z, y_lo, 1 - core


def pair_chip(y_hi, x, z, y_lo, core):
    return y_hi, x, z, 1 - y_lo, core


def across_y(y_hi, x, z, y_lo, core):
    return 1 - y_hi, x, z, 1 - y_lo, core


def other_pair(y_hi, x, z, y_lo, core):
    return y_hi, x, z, 1 - y_lo, 1 - core


OWNERS = (other_core, pair_chip, other_pair)


def spread(value, axes, members):
    copies = jnp.broadcast_to(value[None], (members,) + value.shape)
    return lax.all_to_all(copies, axes, 0, 0, tiled=True)


def rope_tables():
    exponent = jnp.arange(HEAD_SIZE // 2, dtype=jnp.float32) * (2.0 / HEAD_SIZE)
    inverse = jnp.power(jnp.float32(500000.0), -exponent)
    position = (PREFIX + jnp.arange(ROWS)).astype(jnp.float32)
    angles = position[:, None] * inverse[None, :]
    cosine, sine = jnp.cos(angles), jnp.sin(angles)
    return (
        jnp.concatenate([cosine, cosine], axis=1),
        jnp.concatenate([-sine, sine], axis=1),
    )


def dot(a, b, a_dim, b_dim):
    return lax.dot_general(
        a, b, (((a_dim,), (b_dim,)), ((), ())), preferred_element_type=jnp.float32
    )


def norm_kernel(states, gain, normed):
    wide = states[0].astype(jnp.float32)
    scale = lax.rsqrt(jnp.mean(wide * wide, axis=1, keepdims=True) + 1e-05)
    normed[...] = (wide * scale * gain[...]).astype(jnp.bfloat16)


def normalise(hidden, gain):
    return pl.pallas_call(
        norm_kernel,
        grid=(8,),
        in_specs=[
            pl.BlockSpec((1, 32, WIDTH), lambda i: (0, i, 0)),
            pl.BlockSpec((1, WIDTH), lambda i: (0, 0)),
        ],
        out_specs=pl.BlockSpec((32, WIDTH), lambda i: (i, 0)),
        out_shape=jax.ShapeDtypeStruct((ROWS, WIDTH), jnp.bfloat16),
    )(hidden, gain.reshape(1, WIDTH))


def live(length):
    return lax.broadcasted_iota(jnp.int32, (ROWS, 512), 0) < length


def pack_kernel(place, cotangent, key_rows, value_rows, *packed):
    for index in range(4):

        @pl.when(pl.program_id(0) == index)
        def _():
            target = packed[index]
            target[0:ROWS, :] = jnp.where(live(place[4]), cotangent[0], 0).astype(jnp.bfloat16)
            for half in range(2):
                rows = slice(half * 64, half * 64 + 64)
                target[ROWS:, half * 128 : half * 128 + 128] = key_rows[rows, :].astype(
                    jnp.bfloat16
                )
                target[ROWS:, 256 + half * 128 : 384 + half * 128] = value_rows[rows, :].astype(
                    jnp.bfloat16
                )


def pack(place, cotangent, cartridge):
    return pl.pallas_call(
        pack_kernel,
        grid_spec=pltpu.PrefetchScalarGridSpec(
            num_scalar_prefetch=1,
            grid=(4,),
            in_specs=[
                pl.BlockSpec((1, ROWS, 512), lambda i, place: (0, 0, place[0] ^ i)),
                pl.BlockSpec((128, 128), lambda i, place: (0, place[0] ^ i)),
                pl.BlockSpec((128, 128), lambda i, place: (0, 4 + (place[0] ^ i))),
            ],
            out_specs=[pl.BlockSpec((320, 512), lambda i, place: (0, 0))] * 4,
        ),
        out_shape=[jax.ShapeDtypeStruct((320, 512), jnp.bfloat16)] * 4,
    )(place, cotangent, cartridge, cartridge)


def unpack_kernel(place, *refs):
    out = refs[4]
    for index in range(4):

        @pl.when(pl.program_id(0) == index)
        def _():
            out[0] = jnp.where(live(place[4]), refs[index][...], 0).astype(jnp.bfloat16)


def unpack(place, pieces):
    return pl.pallas_call(
        unpack_kernel,
        grid_spec=pltpu.PrefetchScalarGridSpec(
            num_scalar_prefetch=1,
            grid=(4,),
            in_specs=[pl.BlockSpec((ROWS, 512), lambda i, place: (0, 0))] * 4,
            out_specs=pl.BlockSpec((1, ROWS, 512), lambda i, place: (0, 0, place[0] ^ i)),
        ),
        out_shape=jax.ShapeDtypeStruct((1, ROWS, 2048), jnp.bfloat16),
    )(place, *pieces)


def layer_kernel(place, *refs):
    states = refs[0:4]
    z_pieces = refs[4:12]
    x_pieces = refs[12:20]
    packed, cosine, sine = refs[20:24], refs[24], refs[25]
    outs, gradient = refs[26:30], refs[30]
    weights, rows, keys, values, ups, out, sums, piece_sem, row_sem, up_sem = refs[31:]
    step = pl.program_id(0)
    y_hi, x, z = place[1], place[2], place[3]

    def piece_copies():
        copies = []

        def add(source, target):
            copies.append(
                pltpu.make_async_copy(source, target, piece_sem.at[len(copies)])
            )

        offsets = (0, -1, 1, -2, 2, -3, 3, 4)
        for piece, offset in zip(z_pieces, offsets):
            z_from = lax.rem(z + (offset + Z_SIZE), Z_SIZE)
            for back in range(X_SIZE):
                x_from = lax.rem(x + (X_SIZE - back), X_SIZE)
                add(piece.at[back], weights.at[:, x_from, z_from, :, pl.ds(0, HALF)])
        for index, offset in enumerate((0, -1, 1, 2)):
            x_from = lax.rem(x + (offset + X_SIZE), X_SIZE)
            for order in range(Z_SIZE):
                z_from = lax.rem(z + (offsets[order] + Z_SIZE), Z_SIZE)
                piece = x_pieces[2 * index + (order >= 3)]
                add(
                    piece.at[order - 3 if order >= 3 else order],
                    weights.at[:, x_from, z_from, :, pl.ds(HALF, HALF)],
                )
        return copies

    def row_copy(index):
        slot = index % 2
        return pltpu.make_async_copy(states[index], rows.at[slot], row_sem.at[slot])

    def up_copies():
        return [
            pltpu.make_async_copy(packed[index], ups.at[index], up_sem.at[index])
            for index in range(4)
        ]

    @pl.when(step == 0)
    def _():
        for copy in piece_copies():
            copy.start()
        row_copy(0).start()
        row_copy(1).start()
        for copy in up_copies():
            copy.start()
        sums[...] = jnp.zeros_like(sums)
        for copy in up_copies():
            copy.wait()
        for index in range(4):
            first = pl.multiple_of((place[0] ^ index) * 128, 128)
            for half in range(2):
                target = pl.ds(first + half * 64, 64)
                keys[target, :] = ups[index, ROWS:, half * 128 : half * 128 + 128]
                values[target, :] = ups[index, ROWS:, 256 + half * 128 : 384 + half * 128]
        for copy in piece_copies():
            copy.wait()

    for index in range(4):

        @pl.when(step == index)
        def _():
            if index in (1, 2):
                row_copy(index + 1).start()
            row_copy(index).wait()

    slot = lax.rem(step, 2)
    projected = sum(
        dot(
            rows[slot, :, pl.ds(pl.multiple_of((y_hi ^ side) * 2048, 2048), 2048)],
            weights[side].reshape(2048, COLS),
            1,
            0,
        )
        for side in range(2)
    )
    cos, sin = cosine[...], sine[...]

    def rope(v):
        return (v * cos + pltpu.roll(v, HEAD_SIZE // 2, 1) * sin).astype(jnp.bfloat16)

    own_keys = rope(projected[:, 512:640])
    own_values = projected[:, 640:768].astype(jnp.bfloat16)
    prefix_keys, prefix_values = keys[...], values[...]
    causal = lax.broadcasted_iota(jnp.int32, (ROWS, ROWS), 0) >= lax.broadcasted_iota(
        jnp.int32, (ROWS, ROWS), 1
    )
    scale = HEAD_SIZE ** (-0.5) * LOG2E
    key_sum = jnp.zeros((HEAD_SIZE, PREFIX), jnp.float32)
    value_sum = jnp.zeros((HEAD_SIZE, PREFIX), jnp.float32)
    for head in range(GROUP):
        lanes = slice(head * HEAD_SIZE, (head + 1) * HEAD_SIZE)
        query = rope(projected[:, lanes])
        upstream = ups[step, 0:ROWS, lanes]
        before = dot(query, prefix_keys, 1, 1) * scale
        own = jnp.where(causal, dot(query, own_keys, 1, 1) * scale, -1e30)
        highest = jnp.maximum(
            jnp.max(before, axis=1, keepdims=True), jnp.max(own, axis=1, keepdims=True)
        )
        before = jnp.exp2(before - highest)
        own = jnp.exp2(own - highest)
        total = jnp.sum(before, axis=1, keepdims=True) + jnp.sum(own, axis=1, keepdims=True)
        inverse = 1.0 / total
        probs = before * inverse
        probs_low = probs.astype(jnp.bfloat16)
        own_low = (own * inverse).astype(jnp.bfloat16)
        attended = (
            dot(probs_low, prefix_values, 1, 0) + dot(own_low, own_values, 1, 0)
        ).astype(jnp.bfloat16)
        out[:, lanes] = attended
        delta = jnp.sum(
            upstream.astype(jnp.float32) * attended.astype(jnp.float32),
            axis=1,
            keepdims=True,
        )
        dprob = dot(upstream, prefix_values, 1, 1)
        dscore = (probs * (dprob - delta)).astype(jnp.bfloat16)
        key_sum += dot(query, dscore, 0, 0)
        value_sum += dot(upstream, probs_low, 0, 0)
    sums[0:HEAD_SIZE, :] += key_sum * HEAD_SIZE ** (-0.5)
    sums[HEAD_SIZE:, :] += value_sum

    for index in range(4):

        @pl.when(step == index)
        def _():
            outs[index][...] = out[...]

    @pl.when(step == 3)
    def _():
        gradient[...] = sums[...].T.astype(gradient.dtype)


def layer(place, states, z_pieces, x_pieces, packed, cosine, sine):
    anywhere = pl.BlockSpec(memory_space=pl.ANY)

    def whole(shape):
        return pl.BlockSpec(
            shape, lambda i, place: (0,) * len(shape), pipeline_mode=pl.Buffered(1)
        )

    return pl.pallas_call(
        layer_kernel,
        grid_spec=pltpu.PrefetchScalarGridSpec(
            num_scalar_prefetch=1,
            grid=(4,),
            in_specs=[anywhere] * 24 + [whole(cosine.shape), whole(sine.shape)],
            out_specs=[pl.BlockSpec((ROWS, 512), lambda i, place: (0, 0))] * 4
            + [
                pl.BlockSpec((PREFIX, 256), lambda i, place: (0, 0)),
            ],
            scratch_shapes=[
                pltpu.VMEM((2, X_SIZE, Z_SIZE, 64, COLS), jnp.bfloat16),
                pltpu.VMEM((2, ROWS, WIDTH), jnp.bfloat16),
                pltpu.VMEM((PREFIX, HEAD_SIZE), jnp.bfloat16),
                pltpu.VMEM((PREFIX, HEAD_SIZE), jnp.bfloat16),
                pltpu.VMEM((4, 320, 512), jnp.bfloat16),
                pltpu.VMEM((ROWS, 512), jnp.bfloat16),
                pltpu.VMEM((256, PREFIX), jnp.float32),
                pltpu.SemaphoreType.DMA((64,)),
                pltpu.SemaphoreType.DMA((2,)),
                pltpu.SemaphoreType.DMA((4,)),
            ],
        ),
        out_shape=[jax.ShapeDtypeStruct((ROWS, 512), jnp.bfloat16)] * 4
        + [
            jax.ShapeDtypeStruct((PREFIX, 256), jnp.bfloat16),
        ],
        compiler_params=pltpu.CompilerParams(dimension_semantics=("arbitrary",)),
    )(place, *states, *z_pieces, *x_pieces, *packed, cosine, sine)


def of_head(query_weight, key_value_weight, index):
    return jnp.concatenate(
        [
            lax.dynamic_slice_in_dim(query_weight, index * 512, 512, 1),
            lax.dynamic_slice_in_dim(key_value_weight, index * 128, 128, 1),
            lax.dynamic_slice_in_dim(key_value_weight, 512 + index * 128, 128, 1),
        ],
        axis=1,
    )


def gather_weights(own, across):
    both = jnp.stack([own, across])
    first, second = both[:, :, :HALF], both[:, :, HALF:]
    ups, downs = [second], [second]
    for _ in range(3):
        ups.append(permute(ups[-1], along_z(1)))
        downs.append(permute(downs[-1], along_z(-1)))
    last = permute(ups[3], along_z(1))
    near = jnp.stack([second, ups[1], downs[1]])
    rest = jnp.stack([ups[2], downs[2], ups[3], downs[3], last])
    near_up, near_down = permute(near, along_x(1)), permute(near, along_x(-1))
    rest_up, rest_down = permute(rest, along_x(1)), permute(rest, along_x(-1))
    near_two = permute(near_up, along_x(1))
    rest_two = permute(rest_down, along_x(-1))
    x_pieces = [near, rest, near_up, rest_up, near_down, rest_down, near_two, rest_two]
    block = jnp.stack([first] + [permute(first, along_x(step)) for step in (1, 2, 3)])
    z_pieces = [block]
    up, down = block, block
    for _ in range(3):
        up, down = permute(up, along_z(1)), permute(down, along_z(-1))
        z_pieces += [up, down]
    z_pieces += [permute(up, along_z(1))]
    return z_pieces, x_pieces


def adam_update(current, moment_one, moment_two, prefix_gradient):
    one_new = 0.9 * moment_one + 0.1 * prefix_gradient
    two_new = 0.999 * moment_two + 0.001 * prefix_gradient * prefix_gradient
    one_fix = 1.0 - 0.9**STEP
    two_fix = 1.0 - 0.999**STEP
    updated = current - 0.02 * (one_new / one_fix) / (jnp.sqrt(two_new / two_fix) + 1e-08)
    return (updated, one_new, two_new)


def layer_step(
    hidden,
    norm_gain,
    query_weight,
    key_value_weight,
    lengths,
    cotangent,
    cartridge,
    adam_first_moment,
    adam_second_moment,
):
    head = lax.axis_index("owner")
    replica = lax.axis_index("dp")
    cosine, sine = rope_tables()
    place = jnp.stack(
        [head, lax.axis_index("fsdp"), replica // Z_SIZE, replica % Z_SIZE, lengths[0]]
    ).astype(jnp.int32)
    sent = of_head(query_weight, key_value_weight, head ^ 2)
    own = of_head(query_weight, key_value_weight, head)
    own, sent, hidden = lax.optimization_barrier((own, sent, hidden))
    across = permute(sent, across_y)
    normed = normalise(hidden, norm_gain)
    far = permute(normed, pair_chip)
    near = permute(normed, other_core)
    z_pieces, x_pieces = gather_weights(own, across)
    packed = pack(place, cotangent, cartridge)
    packed = [packed[0]] + [permute(packed[i], OWNERS[i - 1]) for i in (1, 2, 3)]
    far, z_pieces[5], z_pieces[6] = lax.optimization_barrier((far, z_pieces[5], z_pieces[6]))
    farthest = permute(far, other_core)
    *attended, gradient = layer(
        place, (normed, near, far, farthest), z_pieces, x_pieces, packed, cosine, sine
    )

    returned = [attended[0]] + [permute(v, m) for v, m in zip(attended[1:], OWNERS)]
    terms = lax.all_to_all(gradient.reshape(256, 2, 256), ("owner", "fsdp", "dp"), 0, 0, tiled=True)
    summed = jnp.sum(terms.reshape(4, 64, 2, 2, 128).astype(jnp.float32), axis=1)
    summed = summed.transpose(1, 2, 0, 3).reshape(2, 1024)
    owned = spread(summed.astype(jnp.bfloat16), ("fsdp", "dp"), 64)
    owned = owned.reshape(128, 1024).astype(jnp.float32)
    attention_out = unpack(place, returned)
    new_cartridge, new_first, new_second = adam_update(
        cartridge, adam_first_moment, adam_second_moment, owned
    )
    return attention_out, new_cartridge, new_first, new_second


def solution(mesh):
    placed = (
        P(MESH_AXES, None, None),
        P(),
        P(("fsdp", "dp"), None),
        P(("fsdp", "dp"), None),
        P(MESH_AXES),
        P(MESH_AXES, None, None),
        P("owner", None),
        P("owner", None),
        P("owner", None),
    )
    return jax.shard_map(
        layer_step,
        mesh=mesh,
        in_specs=placed,
        out_specs=(
            P(MESH_AXES, None, None),
            P("owner", None),
            P("owner", None),
            P("owner", None),
        ),
        check_vma=False,
    )
```

```python
import jax
import jax.numpy as jnp
from jax import lax
from jax.experimental import pallas as pl
from jax.experimental.pallas import tpu as pltpu
from jax.sharding import PartitionSpec as P


HEAD_SIZE = 128
GROUP = 4
STEP = 50
ROWS = 256
WIDTH = 4096
PREFIX = 512
COLS = 768
HALF = 384
MESH_AXES = ("fsdp", "dp", "owner")
X_SIZE, Z_SIZE = 4, 8
LOG2E = 1.4426950408889634


def coords(i):
    return i // 128, (i % 128) // 32, (i // 4) % 8, (i // 2) % 2, i % 2


def device_at(y_hi, x, z, y_lo, core):
    return y_hi * 128 + (x * 8 + z) * 4 + y_lo * 2 + core


def permute(value, move):
    pairs = [(i, device_at(*move(*coords(i)))) for i in range(256)]
    return lax.ppermute(value, MESH_AXES, pairs)


def along_z(step):
    return lambda y_hi, x, z, y_lo, core: (y_hi, x, (z + step) % Z_SIZE, y_lo, core)


def along_x(step):
    return lambda y_hi, x, z, y_lo, core: (y_hi, (x + step) % X_SIZE, z, y_lo, core)


def other_core(y_hi, x, z, y_lo, core):
    return y_hi, x, z, y_lo, 1 - core


def pair_chip(y_hi, x, z, y_lo, core):
    return y_hi, x, z, 1 - y_lo, core


def across_y(y_hi, x, z, y_lo, core):
    return 1 - y_hi, x, z, 1 - y_lo, core


def spread(value, axes, members):
    copies = jnp.broadcast_to(value[None], (members,) + value.shape)
    return lax.all_to_all(copies, axes, 0, 0, tiled=True)


def rope_tables():
    exponent = jnp.arange(HEAD_SIZE // 2, dtype=jnp.float32) * (2.0 / HEAD_SIZE)
    inverse = jnp.power(jnp.float32(500000.0), -exponent)
    position = (PREFIX + jnp.arange(ROWS)).astype(jnp.float32)
    angles = position[:, None] * inverse[None, :]
    cosine, sine = jnp.cos(angles), jnp.sin(angles)
    return (
        jnp.concatenate([cosine, cosine], axis=1),
        jnp.concatenate([-sine, sine], axis=1),
    )


def dot(a, b, a_dim, b_dim):
    return lax.dot_general(
        a, b, (((a_dim,), (b_dim,)), ((), ())), preferred_element_type=jnp.float32
    )


def norm_kernel(states, gain, normed):
    wide = states[0].astype(jnp.float32)
    scale = lax.rsqrt(jnp.mean(wide * wide, axis=1, keepdims=True) + 1e-05)
    normed[...] = (wide * scale * gain[...]).astype(jnp.bfloat16)


def normalise(hidden, gain, half):
    return pl.pallas_call(
        norm_kernel,
        grid=(2,),
        in_specs=[
            pl.BlockSpec((1, 64, WIDTH), lambda i: (0, 2 * half + i, 0)),
            pl.BlockSpec((1, WIDTH), lambda i: (0, 0)),
        ],
        out_specs=pl.BlockSpec((64, WIDTH), lambda i: (i, 0)),
        out_shape=jax.ShapeDtypeStruct((ROWS // 2, WIDTH), jnp.bfloat16),
    )(hidden, gain.reshape(1, WIDTH))


def live(length):
    return lax.broadcasted_iota(jnp.int32, (ROWS, 512), 0) < length


def pack_kernel(place, cotangent, key_rows, value_rows, *packed):
    for index in range(4):

        @pl.when(pl.program_id(0) == index)
        def _():
            target = packed[index] if index < 2 else packed[2].at[index - 2]
            target[0:ROWS, :] = jnp.where(live(place[4]), cotangent[0], 0).astype(jnp.bfloat16)
            for half in range(2):
                rows = slice(half * 64, half * 64 + 64)
                target[ROWS:, half * 128 : half * 128 + 128] = key_rows[rows, :].astype(
                    jnp.bfloat16
                )
                target[ROWS:, 256 + half * 128 : 384 + half * 128] = value_rows[rows, :].astype(
                    jnp.bfloat16
                )


def pack(place, cotangent, cartridge):
    return pl.pallas_call(
        pack_kernel,
        grid_spec=pltpu.PrefetchScalarGridSpec(
            num_scalar_prefetch=1,
            grid=(4,),
            in_specs=[
                pl.BlockSpec((1, ROWS, 512), lambda i, place: (0, 0, place[0] ^ i)),
                pl.BlockSpec((128, 128), lambda i, place: (0, place[0] ^ i)),
                pl.BlockSpec((128, 128), lambda i, place: (0, 4 + (place[0] ^ i))),
            ],
            out_specs=[pl.BlockSpec((320, 512), lambda i, place: (0, 0))] * 2
            + [pl.BlockSpec((2, 320, 512), lambda i, place: (0, 0, 0))],
        ),
        out_shape=[jax.ShapeDtypeStruct((320, 512), jnp.bfloat16)] * 2
        + [jax.ShapeDtypeStruct((2, 320, 512), jnp.bfloat16)],
    )(place, cotangent, cartridge, cartridge)


def unpack_kernel(place, *refs):
    out = refs[4]
    for index in range(4):

        @pl.when(pl.program_id(0) == index)
        def _():
            out[0] = jnp.where(live(place[4]), refs[index][...], 0).astype(jnp.bfloat16)


def unpack(place, pieces):
    return pl.pallas_call(
        unpack_kernel,
        grid_spec=pltpu.PrefetchScalarGridSpec(
            num_scalar_prefetch=1,
            grid=(4,),
            in_specs=[pl.BlockSpec((ROWS, 512), lambda i, place: (0, 0))] * 2
            + [
                pl.BlockSpec((None, ROWS, 512), lambda i, place: (0, 0, 0)),
                pl.BlockSpec((None, ROWS, 512), lambda i, place: (1, 0, 0)),
            ],
            out_specs=pl.BlockSpec((1, ROWS, 512), lambda i, place: (0, 0, place[0] ^ i)),
        ),
        out_shape=jax.ShapeDtypeStruct((1, ROWS, 2048), jnp.bfloat16),
    )(place, *pieces)


def layer_kernel(place, *refs):
    states = refs[0:8]
    z_pieces = refs[8:16]
    x_pieces = refs[16:24]
    packed, cosine, sine = refs[24:28], refs[28], refs[29]
    outs, gradient = refs[30:33], refs[33]
    weights, rows, keys, values, ups, out, sums, piece_sem, row_sem, up_sem = refs[34:]
    step = pl.program_id(0)
    y_hi, x, z = place[1], place[2], place[3]

    def piece_copies():
        copies = []

        def add(source, target):
            copies.append(
                pltpu.make_async_copy(source, target, piece_sem.at[len(copies)])
            )

        offsets = (0, -1, 1, -2, 2, -3, 3, 4)
        for piece, offset in zip(z_pieces, offsets):
            z_from = lax.rem(z + (offset + Z_SIZE), Z_SIZE)
            for back in range(X_SIZE):
                x_from = lax.rem(x + (X_SIZE - back), X_SIZE)
                add(piece.at[back], weights.at[:, x_from, z_from, :, pl.ds(0, HALF)])
        for index, offset in enumerate((0, -1, 1, 2)):
            x_from = lax.rem(x + (offset + X_SIZE), X_SIZE)
            for order in range(Z_SIZE):
                z_from = lax.rem(z + (offsets[order] + Z_SIZE), Z_SIZE)
                piece = x_pieces[2 * index + (order >= 3)]
                add(
                    piece.at[order - 3 if order >= 3 else order],
                    weights.at[:, x_from, z_from, :, pl.ds(HALF, HALF)],
                )
        return copies

    def row_copies(index):
        slot = index % 2
        return [
            pltpu.make_async_copy(
                states[2 * index + half],
                rows.at[slot, pl.ds(half * 128, 128)],
                row_sem.at[slot, half],
            )
            for half in range(2)
        ]

    def up_copies():
        return [
            pltpu.make_async_copy(source, ups.at[index], up_sem.at[index])
            for index, source in enumerate(
                (packed[0], packed[1], packed[2].at[0], packed[3].at[1])
            )
        ]

    @pl.when(step == 0)
    def _():
        for copy in piece_copies():
            copy.start()
        for copy in row_copies(0) + row_copies(1):
            copy.start()
        for copy in up_copies():
            copy.start()
        sums[...] = jnp.zeros_like(sums)
        for copy in up_copies():
            copy.wait()
        for index in range(4):
            first = pl.multiple_of((place[0] ^ index) * 128, 128)
            for half in range(2):
                target = pl.ds(first + half * 64, 64)
                keys[target, :] = ups[index, ROWS:, half * 128 : half * 128 + 128]
                values[target, :] = ups[index, ROWS:, 256 + half * 128 : 384 + half * 128]
        for copy in piece_copies():
            copy.wait()

    for index in range(4):

        @pl.when(step == index)
        def _():
            if index in (1, 2):
                for copy in row_copies(index + 1):
                    copy.start()
            for copy in row_copies(index):
                copy.wait()

    slot = lax.rem(step, 2)
    projected = sum(
        dot(
            rows[slot, :, pl.ds(pl.multiple_of((y_hi ^ side) * 2048, 2048), 2048)],
            weights[side].reshape(2048, COLS),
            1,
            0,
        )
        for side in range(2)
    )
    cos, sin = cosine[...], sine[...]

    def rope(v):
        return (v * cos + pltpu.roll(v, HEAD_SIZE // 2, 1) * sin).astype(jnp.bfloat16)

    own_keys = rope(projected[:, 512:640])
    own_values = projected[:, 640:768].astype(jnp.bfloat16)
    prefix_keys, prefix_values = keys[...], values[...]
    causal = lax.broadcasted_iota(jnp.int32, (ROWS, ROWS), 0) >= lax.broadcasted_iota(
        jnp.int32, (ROWS, ROWS), 1
    )
    scale = HEAD_SIZE ** (-0.5) * LOG2E
    lanes = [slice(h * HEAD_SIZE, (h + 1) * HEAD_SIZE) for h in range(GROUP)]
    queries = [rope(projected[:, lane]) for lane in lanes]
    key_sum = jnp.zeros((HEAD_SIZE, PREFIX), jnp.float32)
    value_sum = jnp.zeros((HEAD_SIZE, PREFIX), jnp.float32)

    def scores(head):
        return dot(queries[head], prefix_keys, 1, 1), dot(queries[head], own_keys, 1, 1)

    def soft(ready):
        before, own = ready
        own = jnp.where(causal, own, -1e30)
        highest = jnp.maximum(
            jnp.max(before, axis=1, keepdims=True), jnp.max(own, axis=1, keepdims=True)
        )
        before = jnp.exp2((before - highest) * scale)
        own = jnp.exp2((own - highest) * scale)
        total = jnp.sum(before, axis=1, keepdims=True) + jnp.sum(own, axis=1, keepdims=True)
        inverse = 1.0 / total
        probs = before * inverse
        return probs, probs.astype(jnp.bfloat16), (own * inverse).astype(jnp.bfloat16)

    def attend(head, soft_out):
        _, probs_low, own_low = soft_out
        upstream = ups[step, 0:ROWS, lanes[head]]
        attended = (
            dot(probs_low, prefix_values, 1, 0) + dot(own_low, own_values, 1, 0)
        ).astype(jnp.bfloat16)
        out[:, lanes[head]] = attended
        return attended, dot(upstream, prefix_values, 1, 1), dot(upstream, probs_low, 0, 0)

    def back(head, probs, attended, dprob):
        upstream = ups[step, 0:ROWS, lanes[head]]
        delta = jnp.sum(
            upstream.astype(jnp.float32) * attended.astype(jnp.float32),
            axis=1,
            keepdims=True,
        )
        dscore = (probs * (dprob - delta)).astype(jnp.bfloat16)
        return dot(queries[head], dscore, 0, 0)

    score_out, soft_out, attend_out = {}, {}, {}
    for tick in range(GROUP + 3):
        if tick < GROUP:
            score_out[tick] = scores(tick)
        if 0 <= tick - 2 < GROUP:
            attend_out[tick - 2] = attend(tick - 2, soft_out[tick - 2])
            value_sum += attend_out[tick - 2][2]
        if 0 <= tick - 1 < GROUP:
            soft_out[tick - 1] = soft(score_out[tick - 1])
        if 0 <= tick - 3 < GROUP:
            attended, dprob, _ = attend_out[tick - 3]
            key_sum += back(tick - 3, soft_out[tick - 3][0], attended, dprob)
    sums[0:HEAD_SIZE, :] += key_sum * HEAD_SIZE ** (-0.5)
    sums[HEAD_SIZE:, :] += value_sum

    for index in range(4):

        @pl.when(step == index)
        def _():
            target = outs[index] if index < 2 else outs[2].at[index - 2]
            target[...] = out[...]

    @pl.when(step == 3)
    def _():
        gradient[...] = sums[...].T.astype(gradient.dtype)


def layer(place, states, z_pieces, x_pieces, packed, cosine, sine):
    anywhere = pl.BlockSpec(memory_space=pl.ANY)

    def whole(shape):
        return pl.BlockSpec(
            shape, lambda i, place: (0,) * len(shape), pipeline_mode=pl.Buffered(1)
        )

    return pl.pallas_call(
        layer_kernel,
        grid_spec=pltpu.PrefetchScalarGridSpec(
            num_scalar_prefetch=1,
            grid=(4,),
            in_specs=[anywhere] * 28 + [whole(cosine.shape), whole(sine.shape)],
            out_specs=[pl.BlockSpec((ROWS, 512), lambda i, place: (0, 0))] * 2
            + [
                pl.BlockSpec((2, ROWS, 512), lambda i, place: (0, 0, 0)),
                pl.BlockSpec((PREFIX, 256), lambda i, place: (0, 0)),
            ],
            scratch_shapes=[
                pltpu.VMEM((2, X_SIZE, Z_SIZE, 64, COLS), jnp.bfloat16),
                pltpu.VMEM((2, ROWS, WIDTH), jnp.bfloat16),
                pltpu.VMEM((PREFIX, HEAD_SIZE), jnp.bfloat16),
                pltpu.VMEM((PREFIX, HEAD_SIZE), jnp.bfloat16),
                pltpu.VMEM((4, 320, 512), jnp.bfloat16),
                pltpu.VMEM((ROWS, 512), jnp.bfloat16),
                pltpu.VMEM((256, PREFIX), jnp.float32),
                pltpu.SemaphoreType.DMA((64,)),
                pltpu.SemaphoreType.DMA((2, 2)),
                pltpu.SemaphoreType.DMA((4,)),
            ],
        ),
        out_shape=[jax.ShapeDtypeStruct((ROWS, 512), jnp.bfloat16)] * 2
        + [
            jax.ShapeDtypeStruct((2, ROWS, 512), jnp.bfloat16),
            jax.ShapeDtypeStruct((PREFIX, 256), jnp.bfloat16),
        ],
        compiler_params=pltpu.CompilerParams(dimension_semantics=("arbitrary",)),
    )(place, *states, *z_pieces, *x_pieces, *packed, cosine, sine)


def of_head(query_weight, key_value_weight, index):
    return jnp.concatenate(
        [
            lax.dynamic_slice_in_dim(query_weight, index * 512, 512, 1),
            lax.dynamic_slice_in_dim(key_value_weight, index * 128, 128, 1),
            lax.dynamic_slice_in_dim(key_value_weight, 512 + index * 128, 128, 1),
        ],
        axis=1,
    )


def gather_weights(own, across):
    both = jnp.stack([own, across])
    first, second = both[:, :, :HALF], both[:, :, HALF:]
    ups, downs = [second], [second]
    for _ in range(3):
        ups.append(permute(ups[-1], along_z(1)))
        downs.append(permute(downs[-1], along_z(-1)))
    last = permute(ups[3], along_z(1))
    near = jnp.stack([second, ups[1], downs[1]])
    rest = jnp.stack([ups[2], downs[2], ups[3], downs[3], last])
    near_up, near_down = permute(near, along_x(1)), permute(near, along_x(-1))
    rest_up, rest_down = permute(rest, along_x(1)), permute(rest, along_x(-1))
    near_two = permute(near_up, along_x(1))
    rest_two = permute(rest_down, along_x(-1))
    x_pieces = [near, rest, near_up, rest_up, near_down, rest_down, near_two, rest_two]
    block = jnp.stack([first] + [permute(first, along_x(step)) for step in (1, 2, 3)])
    z_pieces = [block]
    up, down = block, block
    for _ in range(3):
        up, down = permute(up, along_z(1)), permute(down, along_z(-1))
        z_pieces += [up, down]
    z_pieces += [permute(up, along_z(1))]
    return z_pieces, x_pieces


def adam_update(current, moment_one, moment_two, prefix_gradient):
    one_new = 0.9 * moment_one + 0.1 * prefix_gradient
    two_new = 0.999 * moment_two + 0.001 * prefix_gradient * prefix_gradient
    one_fix = 1.0 - 0.9**STEP
    two_fix = 1.0 - 0.999**STEP
    updated = current - 0.02 * (one_new / one_fix) / (jnp.sqrt(two_new / two_fix) + 1e-08)
    return (updated, one_new, two_new)


def layer_step(
    hidden,
    norm_gain,
    query_weight,
    key_value_weight,
    lengths,
    cotangent,
    cartridge,
    adam_first_moment,
    adam_second_moment,
):
    head = lax.axis_index("owner")
    replica = lax.axis_index("dp")
    cosine, sine = rope_tables()
    place = jnp.stack(
        [head, lax.axis_index("fsdp"), replica // Z_SIZE, replica % Z_SIZE, lengths[0]]
    ).astype(jnp.int32)
    sent = of_head(query_weight, key_value_weight, head ^ 2)
    own = of_head(query_weight, key_value_weight, head)
    own, sent, hidden = lax.optimization_barrier((own, sent, hidden))
    across = permute(sent, across_y)
    states = {}
    for half in range(2):
        normed = normalise(hidden, norm_gain, half)
        far = permute(normed, pair_chip)
        states[half] = (normed, permute(normed, other_core), far, permute(far, other_core))
    z_pieces, x_pieces = gather_weights(own, across)
    own_part, near_part, pair_part = pack(place, cotangent, cartridge)
    pair_part = permute(pair_part, pair_chip)
    packed = (own_part, permute(near_part, other_core), pair_part, permute(pair_part, other_core))
    states = [states[half][index] for index in range(4) for half in range(2)]
    own_out, near_out, pair_out, gradient = layer(
        place, states, z_pieces, x_pieces, packed, cosine, sine
    )
    pair_out = permute(pair_out, pair_chip)
    returned = (own_out, permute(near_out, other_core), pair_out, permute(pair_out, other_core))
    terms = lax.all_to_all(gradient.reshape(256, 2, 256), ("owner", "fsdp", "dp"), 0, 0, tiled=True)
    summed = jnp.sum(terms.reshape(4, 64, 2, 2, 128).astype(jnp.float32), axis=1)
    summed = summed.transpose(1, 2, 0, 3).reshape(2, 1024)
    owned = spread(summed.astype(jnp.bfloat16), ("fsdp", "dp"), 64)
    owned = owned.reshape(128, 1024).astype(jnp.float32)
    attention_out = unpack(place, returned)
    new_cartridge, new_first, new_second = adam_update(
        cartridge, adam_first_moment, adam_second_moment, owned
    )
    return attention_out, new_cartridge, new_first, new_second


def solution(mesh):
    placed = (
        P(MESH_AXES, None, None),
        P(),
        P(("fsdp", "dp"), None),
        P(("fsdp", "dp"), None),
        P(MESH_AXES),
        P(MESH_AXES, None, None),
        P("owner", None),
        P("owner", None),
        P("owner", None),
    )
    return jax.shard_map(
        layer_step,
        mesh=mesh,
        in_specs=placed,
        out_specs=(
            P(MESH_AXES, None, None),
            P("owner", None),
            P("owner", None),
            P("owner", None),
        ),
        check_vma=False,
    )
```

```python
import jax
import jax.numpy as jnp
from jax import lax
from jax.experimental import pallas as pl
from jax.experimental.pallas import tpu as pltpu
from jax.sharding import PartitionSpec as P


HEAD_SIZE = 128
GROUP = 4
STEP = 50
ROWS = 256
WIDTH = 4096
PREFIX = 512
COLS = 768
HALF = 384
MESH_AXES = ("fsdp", "dp", "owner")
X_SIZE, Z_SIZE = 4, 8
LOG2E = 1.4426950408889634


def coords(i):
    return i // 128, (i % 128) // 32, (i // 4) % 8, (i // 2) % 2, i % 2


def device_at(y_hi, x, z, y_lo, core):
    return y_hi * 128 + (x * 8 + z) * 4 + y_lo * 2 + core


def permute(value, move):
    pairs = [(i, device_at(*move(*coords(i)))) for i in range(256)]
    return lax.ppermute(value, MESH_AXES, pairs)


def along_z(step):
    return lambda y_hi, x, z, y_lo, core: (y_hi, x, (z + step) % Z_SIZE, y_lo, core)


def along_x(step):
    return lambda y_hi, x, z, y_lo, core: (y_hi, (x + step) % X_SIZE, z, y_lo, core)


def other_core(y_hi, x, z, y_lo, core):
    return y_hi, x, z, y_lo, 1 - core


def pair_chip(y_hi, x, z, y_lo, core):
    return y_hi, x, z, 1 - y_lo, core


def across_y(y_hi, x, z, y_lo, core):
    return 1 - y_hi, x, z, 1 - y_lo, core


def spread(value, axes, members):
    copies = jnp.broadcast_to(value[None], (members,) + value.shape)
    return lax.all_to_all(copies, axes, 0, 0, tiled=True)


def rope_tables():
    exponent = jnp.arange(HEAD_SIZE // 2, dtype=jnp.float32) * (2.0 / HEAD_SIZE)
    inverse = jnp.power(jnp.float32(500000.0), -exponent)
    position = (PREFIX + jnp.arange(ROWS)).astype(jnp.float32)
    angles = position[:, None] * inverse[None, :]
    cosine, sine = jnp.cos(angles), jnp.sin(angles)
    return (
        jnp.concatenate([cosine, cosine], axis=1),
        jnp.concatenate([-sine, sine], axis=1),
    )


def dot(a, b, a_dim, b_dim):
    return lax.dot_general(
        a, b, (((a_dim,), (b_dim,)), ((), ())), preferred_element_type=jnp.float32
    )


def norm_kernel(states, gain, normed):
    wide = states[0].astype(jnp.float32)
    scale = lax.rsqrt(jnp.mean(wide * wide, axis=1, keepdims=True) + 1e-05)
    normed[...] = (wide * scale * gain[...]).astype(jnp.bfloat16)


def normalise(hidden, gain, half):
    return pl.pallas_call(
        norm_kernel,
        grid=(2,),
        in_specs=[
            pl.BlockSpec((1, 64, WIDTH), lambda i: (0, 2 * half + i, 0)),
            pl.BlockSpec((1, WIDTH), lambda i: (0, 0)),
        ],
        out_specs=pl.BlockSpec((64, WIDTH), lambda i: (i, 0)),
        out_shape=jax.ShapeDtypeStruct((ROWS // 2, WIDTH), jnp.bfloat16),
    )(hidden, gain.reshape(1, WIDTH))


def live(length):
    return lax.broadcasted_iota(jnp.int32, (ROWS, 512), 0) < length


def pack_kernel(place, cotangent, key_rows, value_rows, *packed):
    for index in range(4):

        @pl.when(pl.program_id(0) == index)
        def _():
            target = packed[index] if index < 2 else packed[2].at[index - 2]
            target[0:ROWS, :] = jnp.where(live(place[4]), cotangent[0], 0).astype(jnp.bfloat16)
            for half in range(2):
                rows = slice(half * 64, half * 64 + 64)
                target[ROWS:, half * 128 : half * 128 + 128] = key_rows[rows, :].astype(
                    jnp.bfloat16
                )
                target[ROWS:, 256 + half * 128 : 384 + half * 128] = value_rows[rows, :].astype(
                    jnp.bfloat16
                )


def pack(place, cotangent, cartridge):
    return pl.pallas_call(
        pack_kernel,
        grid_spec=pltpu.PrefetchScalarGridSpec(
            num_scalar_prefetch=1,
            grid=(4,),
            in_specs=[
                pl.BlockSpec((1, ROWS, 512), lambda i, place: (0, 0, place[0] ^ i)),
                pl.BlockSpec((128, 128), lambda i, place: (0, place[0] ^ i)),
                pl.BlockSpec((128, 128), lambda i, place: (0, 4 + (place[0] ^ i))),
            ],
            out_specs=[pl.BlockSpec((320, 512), lambda i, place: (0, 0))] * 2
            + [pl.BlockSpec((2, 320, 512), lambda i, place: (0, 0, 0))],
        ),
        out_shape=[jax.ShapeDtypeStruct((320, 512), jnp.bfloat16)] * 2
        + [jax.ShapeDtypeStruct((2, 320, 512), jnp.bfloat16)],
    )(place, cotangent, cartridge, cartridge)


def unpack_kernel(place, *refs):
    out = refs[4]
    for index in range(4):

        @pl.when(pl.program_id(0) == index)
        def _():
            out[0] = jnp.where(live(place[4]), refs[index][...], 0).astype(jnp.bfloat16)


def unpack(place, pieces):
    return pl.pallas_call(
        unpack_kernel,
        grid_spec=pltpu.PrefetchScalarGridSpec(
            num_scalar_prefetch=1,
            grid=(4,),
            in_specs=[pl.BlockSpec((ROWS, 512), lambda i, place: (0, 0))] * 2
            + [
                pl.BlockSpec((None, ROWS, 512), lambda i, place: (0, 0, 0)),
                pl.BlockSpec((None, ROWS, 512), lambda i, place: (1, 0, 0)),
            ],
            out_specs=pl.BlockSpec((1, ROWS, 512), lambda i, place: (0, 0, place[0] ^ i)),
        ),
        out_shape=jax.ShapeDtypeStruct((1, ROWS, 2048), jnp.bfloat16),
    )(place, *pieces)


def layer_kernel(place, *refs):
    states = refs[0:8]
    z_pieces = refs[8:16]
    x_pieces = refs[16:24]
    packed, cosine, sine = refs[24:28], refs[28], refs[29]
    outs, gradient = refs[30:33], refs[33]
    weights, rows, keys, values, ups, out, sums, heads, piece_sem, row_sem, up_sem = refs[34:]
    step = pl.program_id(0)
    y_hi, x, z = place[1], place[2], place[3]

    def piece_copies():
        copies = []

        def add(source, target):
            copies.append(
                pltpu.make_async_copy(source, target, piece_sem.at[len(copies)])
            )

        offsets = (0, -1, 1, -2, 2, -3, 3, 4)
        for piece, offset in zip(z_pieces, offsets):
            z_from = lax.rem(z + (offset + Z_SIZE), Z_SIZE)
            for back in range(X_SIZE):
                x_from = lax.rem(x + (X_SIZE - back), X_SIZE)
                add(piece.at[back], weights.at[:, x_from, z_from, :, pl.ds(0, HALF)])
        for index, offset in enumerate((0, -1, 1, 2)):
            x_from = lax.rem(x + (offset + X_SIZE), X_SIZE)
            for order in range(Z_SIZE):
                z_from = lax.rem(z + (offsets[order] + Z_SIZE), Z_SIZE)
                piece = x_pieces[2 * index + (order >= 3)]
                add(
                    piece.at[order - 3 if order >= 3 else order],
                    weights.at[:, x_from, z_from, :, pl.ds(HALF, HALF)],
                )
        return copies

    def row_copies(index):
        return [
            pltpu.make_async_copy(
                states[2 * index + half],
                rows.at[index, pl.ds(half * 128, 128)],
                row_sem.at[index, half],
            )
            for half in range(2)
        ]

    def up_copies():
        return [
            pltpu.make_async_copy(source, ups.at[index], up_sem.at[index])
            for index, source in enumerate(
                (packed[0], packed[1], packed[2].at[0], packed[3].at[1])
            )
        ]

    def load(first):
        for index in (first, first + 1):
            for copy in row_copies(index):
                copy.wait()

    @pl.when(step == 0)
    def _():
        copies = piece_copies()
        for copy in copies[:32] + row_copies(0) + row_copies(1) + copies[32:]:
            copy.start()
        for copy in up_copies() + row_copies(2) + row_copies(3):
            copy.start()
        sums[...] = jnp.zeros_like(sums)
        load(0)
        for copy in copies:
            copy.wait()

    @pl.when(step == 2)
    def _():
        load(2)

    @pl.when(lax.rem(step, 2) == 0)
    def _():
        def project(block, carry):
            columns = pl.ds(pl.multiple_of(block * 256, 256), 256)
            both = sum(
                dot(
                    rows[
                        pl.ds(step, 2), :, pl.ds(pl.multiple_of((y_hi ^ side) * 2048, 2048), 2048)
                    ].reshape(2 * ROWS, 2048),
                    weights[side, :, :, :, columns].reshape(2048, 256),
                    1,
                    0,
                )
                for side in range(2)
            )
            heads[:, :, columns] = both.reshape(2, ROWS, 256)
            return carry

        lax.fori_loop(0, 3, project, 0)

    @pl.when(step == 0)
    def _():
        for copy in up_copies():
            copy.wait()
        for index in range(4):
            first = pl.multiple_of((place[0] ^ index) * 128, 128)
            for half in range(2):
                target = pl.ds(first + half * 64, 64)
                keys[target, :] = ups[index, ROWS:, half * 128 : half * 128 + 128]
                values[target, :] = ups[index, ROWS:, 256 + half * 128 : 384 + half * 128]

    which = lax.rem(step, 2)
    cos, sin = cosine[...], sine[...]

    def rope(v):
        return (v * cos + pltpu.roll(v, HEAD_SIZE // 2, 1) * sin).astype(jnp.bfloat16)

    own_keys = rope(heads[which, :, 512:640])
    own_values = heads[which, :, 640:768].astype(jnp.bfloat16)
    prefix_keys, prefix_values = keys[...], values[...]
    causal = lax.broadcasted_iota(jnp.int32, (ROWS, ROWS), 0) >= lax.broadcasted_iota(
        jnp.int32, (ROWS, ROWS), 1
    )
    scale = HEAD_SIZE ** (-0.5) * LOG2E
    lanes = [slice(h * HEAD_SIZE, (h + 1) * HEAD_SIZE) for h in range(GROUP)]
    queries = [rope(heads[which, :, lane]) for lane in lanes]
    key_sum = jnp.zeros((HEAD_SIZE, PREFIX), jnp.float32)
    value_sum = jnp.zeros((HEAD_SIZE, PREFIX), jnp.float32)

    def scores(head):
        return dot(queries[head], prefix_keys, 1, 1), dot(queries[head], own_keys, 1, 1)

    def soft(ready):
        before, own = ready
        own = jnp.where(causal, own, -1e30)
        highest = jnp.maximum(
            jnp.max(before, axis=1, keepdims=True), jnp.max(own, axis=1, keepdims=True)
        )
        before = jnp.exp2((before - highest) * scale)
        own = jnp.exp2((own - highest) * scale)
        total = jnp.sum(before, axis=1, keepdims=True) + jnp.sum(own, axis=1, keepdims=True)
        inverse = 1.0 / total
        probs = before * inverse
        return probs, probs.astype(jnp.bfloat16), (own * inverse).astype(jnp.bfloat16)

    def attend(head, soft_out):
        _, probs_low, own_low = soft_out
        upstream = ups[step, 0:ROWS, lanes[head]]
        attended = (
            dot(probs_low, prefix_values, 1, 0) + dot(own_low, own_values, 1, 0)
        ).astype(jnp.bfloat16)
        out[:, lanes[head]] = attended
        return attended, dot(upstream, prefix_values, 1, 1), dot(upstream, probs_low, 0, 0)

    def back(head, probs, attended, dprob):
        upstream = ups[step, 0:ROWS, lanes[head]]
        delta = jnp.sum(
            upstream.astype(jnp.float32) * attended.astype(jnp.float32),
            axis=1,
            keepdims=True,
        )
        dscore = (probs * (dprob - delta)).astype(jnp.bfloat16)
        return dot(queries[head], dscore, 0, 0)

    score_out, soft_out, attend_out = {}, {}, {}
    for tick in range(GROUP + 3):
        if tick < GROUP:
            score_out[tick] = scores(tick)
        if 0 <= tick - 2 < GROUP:
            attend_out[tick - 2] = attend(tick - 2, soft_out[tick - 2])
            value_sum += attend_out[tick - 2][2]
        if 0 <= tick - 1 < GROUP:
            soft_out[tick - 1] = soft(score_out[tick - 1])
        if 0 <= tick - 3 < GROUP:
            attended, dprob, _ = attend_out[tick - 3]
            key_sum += back(tick - 3, soft_out[tick - 3][0], attended, dprob)
    sums[0:HEAD_SIZE, :] += key_sum * HEAD_SIZE ** (-0.5)
    sums[HEAD_SIZE:, :] += value_sum

    for index in range(4):

        @pl.when(step == index)
        def _():
            target = outs[index] if index < 2 else outs[2].at[index - 2]
            target[...] = out[...]

    @pl.when(step == 3)
    def _():
        gradient[...] = sums[...].T.astype(gradient.dtype)


def layer(place, states, z_pieces, x_pieces, packed, cosine, sine):
    anywhere = pl.BlockSpec(memory_space=pl.ANY)

    def whole(shape):
        return pl.BlockSpec(
            shape, lambda i, place: (0,) * len(shape), pipeline_mode=pl.Buffered(1)
        )

    return pl.pallas_call(
        layer_kernel,
        grid_spec=pltpu.PrefetchScalarGridSpec(
            num_scalar_prefetch=1,
            grid=(4,),
            in_specs=[anywhere] * 28 + [whole(cosine.shape), whole(sine.shape)],
            out_specs=[pl.BlockSpec((ROWS, 512), lambda i, place: (0, 0))] * 2
            + [
                pl.BlockSpec((2, ROWS, 512), lambda i, place: (0, 0, 0)),
                pl.BlockSpec((PREFIX, 256), lambda i, place: (0, 0)),
            ],
            scratch_shapes=[
                pltpu.VMEM((2, X_SIZE, Z_SIZE, 64, COLS), jnp.bfloat16),
                pltpu.VMEM((4, ROWS, WIDTH), jnp.bfloat16),
                pltpu.VMEM((PREFIX, HEAD_SIZE), jnp.bfloat16),
                pltpu.VMEM((PREFIX, HEAD_SIZE), jnp.bfloat16),
                pltpu.VMEM((4, 320, 512), jnp.bfloat16),
                pltpu.VMEM((ROWS, 512), jnp.bfloat16),
                pltpu.VMEM((256, PREFIX), jnp.float32),
                pltpu.VMEM((2, ROWS, COLS), jnp.float32),
                pltpu.SemaphoreType.DMA((64,)),
                pltpu.SemaphoreType.DMA((4, 2)),
                pltpu.SemaphoreType.DMA((4,)),
            ],
        ),
        out_shape=[jax.ShapeDtypeStruct((ROWS, 512), jnp.bfloat16)] * 2
        + [
            jax.ShapeDtypeStruct((2, ROWS, 512), jnp.bfloat16),
            jax.ShapeDtypeStruct((PREFIX, 256), jnp.bfloat16),
        ],
        compiler_params=pltpu.CompilerParams(dimension_semantics=("arbitrary",)),
    )(place, *states, *z_pieces, *x_pieces, *packed, cosine, sine)


def of_head(query_weight, key_value_weight, index):
    return jnp.concatenate(
        [
            lax.dynamic_slice_in_dim(query_weight, index * 512, 512, 1),
            lax.dynamic_slice_in_dim(key_value_weight, index * 128, 128, 1),
            lax.dynamic_slice_in_dim(key_value_weight, 512 + index * 128, 128, 1),
        ],
        axis=1,
    )


def gather_weights(own, across):
    both = jnp.stack([own, across])
    first, second = both[:, :, :HALF], both[:, :, HALF:]
    ups, downs = [second], [second]
    for _ in range(3):
        ups.append(permute(ups[-1], along_z(1)))
        downs.append(permute(downs[-1], along_z(-1)))
    last = permute(ups[3], along_z(1))
    near = jnp.stack([second, ups[1], downs[1]])
    rest = jnp.stack([ups[2], downs[2], ups[3], downs[3], last])
    near_up, near_down = permute(near, along_x(1)), permute(near, along_x(-1))
    rest_up, rest_down = permute(rest, along_x(1)), permute(rest, along_x(-1))
    near_two = permute(near_up, along_x(1))
    rest_two = permute(rest_down, along_x(-1))
    x_pieces = [near, rest, near_up, rest_up, near_down, rest_down, near_two, rest_two]
    block = jnp.stack([first] + [permute(first, along_x(step)) for step in (1, 2, 3)])
    z_pieces = [block]
    up, down = block, block
    for _ in range(3):
        up, down = permute(up, along_z(1)), permute(down, along_z(-1))
        z_pieces += [up, down]
    z_pieces += [permute(up, along_z(1))]
    return z_pieces, x_pieces


def adam_update(current, moment_one, moment_two, prefix_gradient):
    one_new = 0.9 * moment_one + 0.1 * prefix_gradient
    two_new = 0.999 * moment_two + 0.001 * prefix_gradient * prefix_gradient
    one_fix = 1.0 - 0.9**STEP
    two_fix = 1.0 - 0.999**STEP
    updated = current - 0.02 * (one_new / one_fix) / (jnp.sqrt(two_new / two_fix) + 1e-08)
    return (updated, one_new, two_new)


def layer_step(
    hidden,
    norm_gain,
    query_weight,
    key_value_weight,
    lengths,
    cotangent,
    cartridge,
    adam_first_moment,
    adam_second_moment,
):
    head = lax.axis_index("owner")
    replica = lax.axis_index("dp")
    cosine, sine = rope_tables()
    place = jnp.stack(
        [head, lax.axis_index("fsdp"), replica // Z_SIZE, replica % Z_SIZE, lengths[0]]
    ).astype(jnp.int32)
    sent = of_head(query_weight, key_value_weight, head ^ 2)
    own = of_head(query_weight, key_value_weight, head)
    own, sent, hidden = lax.optimization_barrier((own, sent, hidden))
    across = permute(sent, across_y)
    states = {}
    for half in range(2):
        normed = normalise(hidden, norm_gain, half)
        far = permute(normed, pair_chip)
        states[half] = (normed, permute(normed, other_core), far, permute(far, other_core))
    z_pieces, x_pieces = gather_weights(own, across)
    own_part, near_part, pair_part = pack(place, cotangent, cartridge)
    pair_part = permute(pair_part, pair_chip)
    packed = (own_part, permute(near_part, other_core), pair_part, permute(pair_part, other_core))
    states = [states[half][index] for index in range(4) for half in range(2)]
    own_out, near_out, pair_out, gradient = layer(
        place, states, z_pieces, x_pieces, packed, cosine, sine
    )
    pair_out = permute(pair_out, pair_chip)
    returned = (own_out, permute(near_out, other_core), pair_out, permute(pair_out, other_core))
    terms = lax.all_to_all(gradient.reshape(256, 2, 256), ("owner", "fsdp", "dp"), 0, 0, tiled=True)
    summed = jnp.sum(terms.reshape(4, 64, 2, 2, 128).astype(jnp.float32), axis=1)
    summed = summed.transpose(1, 2, 0, 3).reshape(2, 1024)
    owned = spread(summed.astype(jnp.bfloat16), ("fsdp", "dp"), 64)
    owned = owned.reshape(128, 1024).astype(jnp.float32)
    attention_out = unpack(place, returned)
    new_cartridge, new_first, new_second = adam_update(
        cartridge, adam_first_moment, adam_second_moment, owned
    )
    return attention_out, new_cartridge, new_first, new_second


def solution(mesh):
    placed = (
        P(MESH_AXES, None, None),
        P(),
        P(("fsdp", "dp"), None),
        P(("fsdp", "dp"), None),
        P(MESH_AXES),
        P(MESH_AXES, None, None),
        P("owner", None),
        P("owner", None),
        P("owner", None),
    )
    return jax.shard_map(
        layer_step,
        mesh=mesh,
        in_specs=placed,
        out_specs=(
            P(MESH_AXES, None, None),
            P("owner", None),
            P("owner", None),
            P("owner", None),
        ),
        check_vma=False,
    )
```

```python
import jax
import jax.numpy as jnp
from jax import lax
from jax.experimental import pallas as pl
from jax.experimental.pallas import tpu as pltpu
from jax.sharding import PartitionSpec as P


HEAD_SIZE = 128
GROUP = 4
STEP = 50
ROWS = 256
WIDTH = 4096
PREFIX = 512
COLS = 768
HALF = 384
MESH_AXES = ("fsdp", "dp", "owner")
X_SIZE, Z_SIZE = 4, 8
LOG2E = 1.4426950408889634


def coords(i):
    return i // 128, (i % 128) // 32, (i // 4) % 8, (i // 2) % 2, i % 2


def device_at(y_hi, x, z, y_lo, core):
    return y_hi * 128 + (x * 8 + z) * 4 + y_lo * 2 + core


def permute(value, move):
    pairs = [(i, device_at(*move(*coords(i)))) for i in range(256)]
    return lax.ppermute(value, MESH_AXES, pairs)


def along_z(step):
    return lambda y_hi, x, z, y_lo, core: (y_hi, x, (z + step) % Z_SIZE, y_lo, core)


def along_x(step):
    return lambda y_hi, x, z, y_lo, core: (y_hi, (x + step) % X_SIZE, z, y_lo, core)


def other_core(y_hi, x, z, y_lo, core):
    return y_hi, x, z, y_lo, 1 - core


def pair_chip(y_hi, x, z, y_lo, core):
    return y_hi, x, z, 1 - y_lo, core


def across_y(y_hi, x, z, y_lo, core):
    return 1 - y_hi, x, z, 1 - y_lo, core


def spread(value, axes, members):
    copies = jnp.broadcast_to(value[None], (members,) + value.shape)
    return lax.all_to_all(copies, axes, 0, 0, tiled=True)


def rope_tables():
    exponent = jnp.arange(HEAD_SIZE // 2, dtype=jnp.float32) * (2.0 / HEAD_SIZE)
    inverse = jnp.power(jnp.float32(500000.0), -exponent)
    position = (PREFIX + jnp.arange(ROWS)).astype(jnp.float32)
    angles = position[:, None] * inverse[None, :]
    cosine, sine = jnp.cos(angles), jnp.sin(angles)
    return (
        jnp.concatenate([cosine, cosine], axis=1),
        jnp.concatenate([-sine, sine], axis=1),
    )


def dot(a, b, a_dim, b_dim):
    return lax.dot_general(
        a, b, (((a_dim,), (b_dim,)), ((), ())), preferred_element_type=jnp.float32
    )


def norm_kernel(states, gain, normed):
    wide = states[0].astype(jnp.float32)
    scale = lax.rsqrt(jnp.mean(wide * wide, axis=1, keepdims=True) + 1e-05)
    normed[...] = (wide * scale * gain[...]).astype(jnp.bfloat16)


def normalise(hidden, gain, half):
    return pl.pallas_call(
        norm_kernel,
        grid=(2,),
        in_specs=[
            pl.BlockSpec((1, 64, WIDTH), lambda i: (0, 2 * half + i, 0)),
            pl.BlockSpec((1, WIDTH), lambda i: (0, 0)),
        ],
        out_specs=pl.BlockSpec((64, WIDTH), lambda i: (i, 0)),
        out_shape=jax.ShapeDtypeStruct((ROWS // 2, WIDTH), jnp.bfloat16),
    )(hidden, gain.reshape(1, WIDTH))


def live(length):
    return lax.broadcasted_iota(jnp.int32, (ROWS, 512), 0) < length


def pack_kernel(place, cotangent, key_rows, value_rows, *packed):
    for index in range(4):

        @pl.when(pl.program_id(0) == index)
        def _():
            target = packed[index] if index < 2 else packed[2].at[index - 2]
            target[0:ROWS, :] = jnp.where(live(place[4]), cotangent[0], 0).astype(jnp.bfloat16)
            for half in range(2):
                rows = slice(half * 64, half * 64 + 64)
                target[ROWS:, half * 128 : half * 128 + 128] = key_rows[rows, :].astype(
                    jnp.bfloat16
                )
                target[ROWS:, 256 + half * 128 : 384 + half * 128] = value_rows[rows, :].astype(
                    jnp.bfloat16
                )


def pack(place, cotangent, cartridge):
    return pl.pallas_call(
        pack_kernel,
        grid_spec=pltpu.PrefetchScalarGridSpec(
            num_scalar_prefetch=1,
            grid=(4,),
            in_specs=[
                pl.BlockSpec((1, ROWS, 512), lambda i, place: (0, 0, place[0] ^ i)),
                pl.BlockSpec((128, 128), lambda i, place: (0, place[0] ^ i)),
                pl.BlockSpec((128, 128), lambda i, place: (0, 4 + (place[0] ^ i))),
            ],
            out_specs=[pl.BlockSpec((320, 512), lambda i, place: (0, 0))] * 2
            + [pl.BlockSpec((2, 320, 512), lambda i, place: (0, 0, 0))],
        ),
        out_shape=[jax.ShapeDtypeStruct((320, 512), jnp.bfloat16)] * 2
        + [jax.ShapeDtypeStruct((2, 320, 512), jnp.bfloat16)],
    )(place, cotangent, cartridge, cartridge)


def unpack_kernel(place, *refs):
    out = refs[4]
    for index in range(4):

        @pl.when(pl.program_id(0) == index)
        def _():
            out[0] = jnp.where(live(place[4]), refs[index][...], 0).astype(jnp.bfloat16)


def unpack(place, pieces):
    return pl.pallas_call(
        unpack_kernel,
        grid_spec=pltpu.PrefetchScalarGridSpec(
            num_scalar_prefetch=1,
            grid=(4,),
            in_specs=[pl.BlockSpec((ROWS, 512), lambda i, place: (0, 0))] * 2
            + [
                pl.BlockSpec((None, ROWS, 512), lambda i, place: (0, 0, 0)),
                pl.BlockSpec((None, ROWS, 512), lambda i, place: (1, 0, 0)),
            ],
            out_specs=pl.BlockSpec((1, ROWS, 512), lambda i, place: (0, 0, place[0] ^ i)),
        ),
        out_shape=jax.ShapeDtypeStruct((1, ROWS, 2048), jnp.bfloat16),
    )(place, *pieces)


def layer_kernel(place, *refs):
    states = refs[0:8]
    z_pieces = refs[8:16]
    x_pieces = refs[16:24]
    packed, cosine, sine = refs[24:28], refs[28], refs[29]
    outs, gradient = refs[30:33], refs[33]
    weights, rows, keys, values, ups, out, sums, heads, piece_sem, row_sem, up_sem = refs[34:]
    step = pl.program_id(0)
    y_hi, x, z = place[1], place[2], place[3]

    def piece_copies():
        copies = []

        def add(source, target):
            copies.append(
                pltpu.make_async_copy(source, target, piece_sem.at[len(copies)])
            )

        offsets = (0, -1, 1, -2, 2, -3, 3, 4)
        for piece, offset in zip(z_pieces, offsets):
            z_from = lax.rem(z + (offset + Z_SIZE), Z_SIZE)
            for back in range(X_SIZE):
                x_from = lax.rem(x + (X_SIZE - back), X_SIZE)
                add(piece.at[back], weights.at[:, x_from, z_from, :, pl.ds(0, HALF)])
        for index, offset in enumerate((0, -1, 1, 2)):
            x_from = lax.rem(x + (offset + X_SIZE), X_SIZE)
            for order in range(Z_SIZE):
                z_from = lax.rem(z + (offsets[order] + Z_SIZE), Z_SIZE)
                piece = x_pieces[2 * index + (order >= 3)]
                add(
                    piece.at[order - 3 if order >= 3 else order],
                    weights.at[:, x_from, z_from, :, pl.ds(HALF, HALF)],
                )
        return copies

    def row_copies(index):
        return [
            pltpu.make_async_copy(
                states[2 * index + half],
                rows.at[index, pl.ds(half * 128, 128)],
                row_sem.at[index, half],
            )
            for half in range(2)
        ]

    def up_copies():
        return [
            pltpu.make_async_copy(source, ups.at[index], up_sem.at[index])
            for index, source in enumerate(
                (packed[0], packed[1], packed[2].at[0], packed[3].at[1])
            )
        ]

    def load(first):
        for index in (first, first + 1):
            for copy in row_copies(index):
                copy.wait()

    @pl.when(step == 0)
    def _():
        copies = piece_copies()
        for copy in copies[:32] + row_copies(0) + row_copies(1) + copies[32:]:
            copy.start()
        for copy in up_copies() + row_copies(2) + row_copies(3):
            copy.start()
        sums[...] = jnp.zeros_like(sums)
        load(0)
        for copy in copies:
            copy.wait()

    @pl.when(step == 2)
    def _():
        load(2)

    @pl.when(lax.rem(step, 2) == 0)
    def _():
        def project(block, carry):
            columns = pl.ds(pl.multiple_of(block * 256, 256), 256)
            both = sum(
                dot(
                    rows[
                        pl.ds(step, 2), :, pl.ds(pl.multiple_of((y_hi ^ side) * 2048, 2048), 2048)
                    ].reshape(2 * ROWS, 2048),
                    weights[side, :, :, :, columns].reshape(2048, 256),
                    1,
                    0,
                )
                for side in range(2)
            )
            heads[:, :, columns] = both.reshape(2, ROWS, 256)
            return carry

        lax.fori_loop(0, 3, project, 0)

    @pl.when(step == 0)
    def _():
        for copy in up_copies():
            copy.wait()
        for index in range(4):
            first = pl.multiple_of((place[0] ^ index) * 128, 128)
            for half in range(2):
                target = pl.ds(first + half * 64, 64)
                keys[target, :] = ups[index, ROWS:, half * 128 : half * 128 + 128]
                values[target, :] = ups[index, ROWS:, 256 + half * 128 : 384 + half * 128]

    which = lax.rem(step, 2)
    cos, sin = cosine[...], sine[...]

    def rope(v):
        return (v * cos + pltpu.roll(v, HEAD_SIZE // 2, 1) * sin).astype(jnp.bfloat16)

    own_keys = rope(heads[which, :, 512:640])
    own_values = heads[which, :, 640:768].astype(jnp.bfloat16)
    prefix_keys, prefix_values = keys[...], values[...]
    causal = lax.broadcasted_iota(jnp.int32, (ROWS, ROWS), 0) >= lax.broadcasted_iota(
        jnp.int32, (ROWS, ROWS), 1
    )
    scale = HEAD_SIZE ** (-0.5) * LOG2E
    lanes = [slice(h * HEAD_SIZE, (h + 1) * HEAD_SIZE) for h in range(GROUP)]
    queries = [rope(heads[which, :, lane]) for lane in lanes]
    key_sum = jnp.zeros((HEAD_SIZE, PREFIX), jnp.float32)
    value_sum = jnp.zeros((HEAD_SIZE, PREFIX), jnp.float32)

    def scores(head):
        return dot(queries[head], prefix_keys, 1, 1), dot(queries[head], own_keys, 1, 1)

    def soft(ready):
        before, own = ready
        own = jnp.where(causal, own, -1e30)
        highest = jnp.maximum(
            jnp.max(before, axis=1, keepdims=True), jnp.max(own, axis=1, keepdims=True)
        )
        before = jnp.exp2((before - highest) * scale)
        own = jnp.exp2((own - highest) * scale)
        total = jnp.sum(before, axis=1, keepdims=True) + jnp.sum(own, axis=1, keepdims=True)
        inverse = 1.0 / total
        probs = before * inverse
        return probs, probs.astype(jnp.bfloat16), (own * inverse).astype(jnp.bfloat16)

    def attend(head, soft_out):
        _, probs_low, own_low = soft_out
        upstream = ups[step, 0:ROWS, lanes[head]]
        attended = (
            dot(probs_low, prefix_values, 1, 0) + dot(own_low, own_values, 1, 0)
        ).astype(jnp.bfloat16)
        out[:, lanes[head]] = attended
        return attended, dot(upstream, prefix_values, 1, 1), dot(upstream, probs_low, 0, 0)

    def back(head, probs, attended, dprob):
        upstream = ups[step, 0:ROWS, lanes[head]]
        delta = jnp.sum(
            upstream.astype(jnp.float32) * attended.astype(jnp.float32),
            axis=1,
            keepdims=True,
        )
        dscore = (probs * (dprob - delta)).astype(jnp.bfloat16)
        return dot(queries[head], dscore, 0, 0)

    score_out, soft_out, attend_out = {}, {}, {}
    for tick in range(GROUP + 4):
        if tick < GROUP:
            score_out[tick] = scores(tick)
        if 0 <= tick - 2 < GROUP:
            attend_out[tick - 2] = attend(tick - 2, soft_out[tick - 2])
            sums[HEAD_SIZE:, :] += attend_out[tick - 2][2]
        if 0 <= tick - 1 < GROUP:
            soft_out[tick - 1] = soft(score_out[tick - 1])
        if 0 <= tick - 4 < GROUP:
            attended, dprob, _ = attend_out[tick - 4]
            sums[0:HEAD_SIZE, :] += back(tick - 4, soft_out[tick - 4][0], attended, dprob) * HEAD_SIZE ** (-0.5)
    for index in range(4):

        @pl.when(step == index)
        def _():
            target = outs[index] if index < 2 else outs[2].at[index - 2]
            target[...] = out[...]

    @pl.when(step == 3)
    def _():
        gradient[...] = sums[...].T.astype(gradient.dtype)


def layer(place, states, z_pieces, x_pieces, packed, cosine, sine):
    anywhere = pl.BlockSpec(memory_space=pl.ANY)

    def whole(shape):
        return pl.BlockSpec(
            shape, lambda i, place: (0,) * len(shape), pipeline_mode=pl.Buffered(1)
        )

    return pl.pallas_call(
        layer_kernel,
        grid_spec=pltpu.PrefetchScalarGridSpec(
            num_scalar_prefetch=1,
            grid=(4,),
            in_specs=[anywhere] * 28 + [whole(cosine.shape), whole(sine.shape)],
            out_specs=[pl.BlockSpec((ROWS, 512), lambda i, place: (0, 0))] * 2
            + [
                pl.BlockSpec((2, ROWS, 512), lambda i, place: (0, 0, 0)),
                pl.BlockSpec((PREFIX, 256), lambda i, place: (0, 0)),
            ],
            scratch_shapes=[
                pltpu.VMEM((2, X_SIZE, Z_SIZE, 64, COLS), jnp.bfloat16),
                pltpu.VMEM((4, ROWS, WIDTH), jnp.bfloat16),
                pltpu.VMEM((PREFIX, HEAD_SIZE), jnp.bfloat16),
                pltpu.VMEM((PREFIX, HEAD_SIZE), jnp.bfloat16),
                pltpu.VMEM((4, 320, 512), jnp.bfloat16),
                pltpu.VMEM((ROWS, 512), jnp.bfloat16),
                pltpu.VMEM((256, PREFIX), jnp.float32),
                pltpu.VMEM((2, ROWS, COLS), jnp.float32),
                pltpu.SemaphoreType.DMA((64,)),
                pltpu.SemaphoreType.DMA((4, 2)),
                pltpu.SemaphoreType.DMA((4,)),
            ],
        ),
        out_shape=[jax.ShapeDtypeStruct((ROWS, 512), jnp.bfloat16)] * 2
        + [
            jax.ShapeDtypeStruct((2, ROWS, 512), jnp.bfloat16),
            jax.ShapeDtypeStruct((PREFIX, 256), jnp.bfloat16),
        ],
        compiler_params=pltpu.CompilerParams(dimension_semantics=("arbitrary",)),
    )(place, *states, *z_pieces, *x_pieces, *packed, cosine, sine)


def of_head(query_weight, key_value_weight, index):
    return jnp.concatenate(
        [
            lax.dynamic_slice_in_dim(query_weight, index * 512, 512, 1),
            lax.dynamic_slice_in_dim(key_value_weight, index * 128, 128, 1),
            lax.dynamic_slice_in_dim(key_value_weight, 512 + index * 128, 128, 1),
        ],
        axis=1,
    )


def gather_weights(own, across):
    both = jnp.stack([own, across])
    first, second = both[:, :, :HALF], both[:, :, HALF:]
    ups, downs = [second], [second]
    for _ in range(3):
        ups.append(permute(ups[-1], along_z(1)))
        downs.append(permute(downs[-1], along_z(-1)))
    last = permute(downs[3], along_z(-1))
    near = jnp.stack([second, ups[1], downs[1]])
    rest = jnp.stack([ups[2], downs[2], ups[3], downs[3], last])
    near_up, near_down = permute(near, along_x(1)), permute(near, along_x(-1))
    rest_up, rest_down = permute(rest, along_x(1)), permute(rest, along_x(-1))
    near_two = permute(near_up, along_x(1))
    rest_two = permute(rest_down, along_x(-1))
    x_pieces = [near, rest, near_up, rest_up, near_down, rest_down, near_two, rest_two]
    block = jnp.stack([first] + [permute(first, along_x(step)) for step in (1, 2, 3)])
    z_pieces = [block]
    up, down = block, block
    for _ in range(3):
        up, down = permute(up, along_z(1)), permute(down, along_z(-1))
        z_pieces += [up, down]
    z_pieces += [permute(up, along_z(1))]
    return z_pieces, x_pieces


def adam_update(current, moment_one, moment_two, prefix_gradient):
    one_new = 0.9 * moment_one + 0.1 * prefix_gradient
    two_new = 0.999 * moment_two + 0.001 * prefix_gradient * prefix_gradient
    one_fix = 1.0 - 0.9**STEP
    two_fix = 1.0 - 0.999**STEP
    updated = current - 0.02 * (one_new / one_fix) / (jnp.sqrt(two_new / two_fix) + 1e-08)
    return (updated, one_new, two_new)


def layer_step(
    hidden,
    norm_gain,
    query_weight,
    key_value_weight,
    lengths,
    cotangent,
    cartridge,
    adam_first_moment,
    adam_second_moment,
):
    head = lax.axis_index("owner")
    replica = lax.axis_index("dp")
    cosine, sine = rope_tables()
    place = jnp.stack(
        [head, lax.axis_index("fsdp"), replica // Z_SIZE, replica % Z_SIZE, lengths[0]]
    ).astype(jnp.int32)
    sent = of_head(query_weight, key_value_weight, head ^ 2)
    own = of_head(query_weight, key_value_weight, head)
    own, sent, hidden = lax.optimization_barrier((own, sent, hidden))
    across = permute(sent, across_y)
    states = {}
    for half in range(2):
        normed = normalise(hidden, norm_gain, half)
        far = permute(normed, pair_chip)
        states[half] = (normed, permute(normed, other_core), far, permute(far, other_core))
    z_pieces, x_pieces = gather_weights(own, across)
    own_part, near_part, pair_part = pack(place, cotangent, cartridge)
    pair_part = permute(pair_part, pair_chip)
    packed = (own_part, permute(near_part, other_core), pair_part, permute(pair_part, other_core))
    states = [states[half][index] for index in range(4) for half in range(2)]
    own_out, near_out, pair_out, gradient = layer(
        place, states, z_pieces, x_pieces, packed, cosine, sine
    )
    pair_out = permute(pair_out, pair_chip)
    returned = (own_out, permute(near_out, other_core), pair_out, permute(pair_out, other_core))
    terms = lax.all_to_all(gradient.reshape(256, 2, 256), ("owner", "fsdp", "dp"), 0, 0, tiled=True)
    summed = jnp.sum(terms.reshape(4, 64, 2, 2, 128).astype(jnp.float32), axis=1)
    summed = summed.transpose(1, 2, 0, 3).reshape(2, 1024)
    owned = spread(summed.astype(jnp.bfloat16), ("fsdp", "dp"), 64)
    owned = owned.reshape(128, 1024).astype(jnp.float32)
    attention_out = unpack(place, returned)
    new_cartridge, new_first, new_second = adam_update(
        cartridge, adam_first_moment, adam_second_moment, owned
    )
    return attention_out, new_cartridge, new_first, new_second


def solution(mesh):
    placed = (
        P(MESH_AXES, None, None),
        P(),
        P(("fsdp", "dp"), None),
        P(("fsdp", "dp"), None),
        P(MESH_AXES),
        P(MESH_AXES, None, None),
        P("owner", None),
        P("owner", None),
        P("owner", None),
    )
    return jax.shard_map(
        layer_step,
        mesh=mesh,
        in_specs=placed,
        out_specs=(
            P(MESH_AXES, None, None),
            P("owner", None),
            P("owner", None),
            P("owner", None),
        ),
        check_vma=False,
    )
```
